512 devices in a mesh: segment: 32 (over y_lo, z), dp: 8 (over x, core), seq: 2 (over y_hi).
Axes of the slice: x: 4, y: 8 (y_hi: 2, y_lo: 4; y = y_hi * 4 + y_lo), z: 8, core: 2. Of those that a mesh axis runs over, the one named last changes fastest.
Arguments:
- stored_part_activation: bfloat16 [32, 2, 8, 256, 2048], P('segment', None, 'dp', 'seq'), may hold values from -64 to 64
- pending_sensitivity: bfloat16 [32, 8, 256, 2048], P('segment', 'dp', 'seq'), may hold values from -0.119628906 to 0.119628906
- uppermost_result_derivative: bfloat16 [1, 8, 256, 2048], P(None, 'dp', 'seq'), may hold values from -0.119628906 to 0.119628906
- scaling_factors: float32 [32, 4, 2048], P('segment'), may hold values from -0.5 to 5
- attended_tile_table: int32 [32, 2, 8, 2, 2], P('segment', None, 'dp'), may hold values from 0 to 1, as said below
- active_tile_number: int32 [32, 2, 8, 2], P('segment', None, 'dp'), may hold values from 1 to 2
Outputs:
- factor_derivatives: float32 [32, 4, 2048], P('segment')
The draws below stay inside these ranges and needn't reach their ends.
Inputs may be any that keep to these rules, and one draw needn't show every extreme that they name: `attended_tile_table`: each list names every key block of its sample once; the allowed ones come first.
All inputs are finite; a program needn't handle non-finite values.
Results may differ from the reference program's by a relative error of at most 0.009.
Values may be sent and summed in bfloat16 or wider, within the bound.
A program may use at most 64 MiB of HBM per device.

```python
import math
import jax
import jax.numpy as jnp
from jax import lax

HEADS = 16
HEAD_DIM = 128
BLK = 128
WINDOW = 2
DEPTH_PARTS = 32
MINIBATCH_SIZE = 8
NBLK = 2
ROWS = 128
SEQUENCE_SPAN = 256
FEATURE_WIDTH = 2048
N_SEQ = 2


def draw_stored_part_activation(key, part):
    base_key, token_key, chan_key = jax.random.split(key, 3)
    full_shape = (DEPTH_PARTS, WINDOW, MINIBATCH_SIZE, SEQUENCE_SPAN, FEATURE_WIDTH)
    base_draw = jax.random.normal(base_key, full_shape, jnp.float32)
    tok_scale = jnp.exp(jax.random.uniform(token_key, full_shape[:-1] + (1,), jnp.float32, math.log(0.3), math.log(3.0)))
    chan_scale = jnp.exp(jax.random.uniform(chan_key, (DEPTH_PARTS, 1, 1, 1, FEATURE_WIDTH), jnp.float32, math.log(0.3), math.log(3.0)))
    values = base_draw * tok_scale * chan_scale
    return jnp.clip(values, -64.0, 64.0).astype(jnp.bfloat16)


def draw_scaling_factors(key, part):
    first_key, second_key, third_key = jax.random.split(key, 3)
    qk_gains = jnp.exp(jax.random.uniform(first_key, (DEPTH_PARTS, 2, FEATURE_WIDTH), jnp.float32, math.log(0.5), math.log(2.0)))
    value_gains = jnp.exp(jax.random.uniform(second_key, (DEPTH_PARTS, 1, FEATURE_WIDTH), jnp.float32, math.log(0.5), math.log(2.0)))
    gate_draw = jax.random.uniform(third_key, (DEPTH_PARTS, 1, FEATURE_WIDTH), jnp.float32, -0.5, 0.5)
    return jnp.concatenate([qk_gains, value_gains, gate_draw], axis=1)


def mask_lists(key):
    mask_key = jax.random.fold_in(key, 4242)
    order_key, count_key = jax.random.split(mask_key)
    leading = (DEPTH_PARTS, WINDOW, MINIBATCH_SIZE, NBLK)
    drawn = jnp.broadcast_to(jnp.arange(NBLK, dtype=jnp.int32), leading + (NBLK,))
    block_list = jax.random.permutation(order_key, drawn, axis=-1, independent=True)
    live_count = jax.random.randint(count_key, leading, 1, NBLK + 1)
    live_count = live_count.at[0, 0, 0, 0].set(NBLK)
    live_count = live_count.at[0, 0, 0, 1].set(1)
    return (block_list.astype(jnp.int32), live_count.astype(jnp.int32))


def draw_attended_tile_table(key, part):
    return mask_lists(key)[0]


def draw_active_tile_number(key, part):
    return mask_lists(key)[1]


def level_of(key, shape, cuts, low, largest):
    gain, own = 1.0, jax.random.fold_in(key, 6)
    for position, blocks in cuts:
        steps = jnp.exp(jax.random.uniform(jax.random.fold_in(own, position), (blocks,), jnp.float32, low / len(cuts), largest / len(cuts)))
        gain = gain * jnp.repeat(steps, shape[position] // blocks).reshape([-1 if axis == position else 1 for axis in range(len(shape))])
    return gain


def bell_draw(key, extent, scale, most, cuts=(), kind=jnp.bfloat16):
    loudness = level_of(key, extent, cuts, -0.22, 0.18) if cuts else 1.0
    entries = jax.random.normal(key, extent, jnp.float32) * scale * loudness
    return jnp.minimum(jnp.maximum(entries, -most), most).astype(kind)


def setup_inputs(seed: int = 0) -> dict:
    arg_keys = jax.random.split(jax.random.key(seed), 7)
    stored_part_activation = draw_stored_part_activation(jax.random.fold_in(arg_keys[6], 71), 0)
    pending_sensitivity = bell_draw(arg_keys[1], (DEPTH_PARTS, MINIBATCH_SIZE, SEQUENCE_SPAN, FEATURE_WIDTH), 0.02, 0.119628906, ((0, 32), (1, 8), (2, 2)))
    uppermost_result_derivative = bell_draw(arg_keys[2], (WINDOW - 1, MINIBATCH_SIZE, SEQUENCE_SPAN, FEATURE_WIDTH), 0.02, 0.119628906, ((1, 8), (2, 2)))
    scaling_factors = draw_scaling_factors(jax.random.fold_in(arg_keys[6], 71), 0)
    attended_tile_table = draw_attended_tile_table(jax.random.fold_in(arg_keys[6], 71), 0)
    active_tile_number = draw_active_tile_number(jax.random.fold_in(arg_keys[6], 71), 0)
    return dict(stored_part_activation=stored_part_activation, pending_sensitivity=pending_sensitivity, uppermost_result_derivative=uppermost_result_derivative, scaling_factors=scaling_factors, attended_tile_table=attended_tile_table, active_tile_number=active_tile_number)


epsilon = 1e-06

def normed_of(inputs):
    widened = inputs.astype(jnp.float32).reshape(inputs.shape[:-1] + (HEADS, HEAD_DIM))
    inv_rms = lax.rsqrt(lax.optimization_barrier(jnp.mean(widened * widened, axis=-1, keepdims=True)) + epsilon)
    return (widened * inv_rms, inv_rms)

def norm_back(grad_norm, norm_val, inv_rms):
    return inv_rms * (grad_norm - norm_val * lax.optimization_barrier(jnp.mean(grad_norm * norm_val, axis=-1, keepdims=True)))

def allowed_blocks(block_list, live_count):
    live_slots = jnp.arange(NBLK)[None, :] < live_count[:, None]
    matches = (block_list[:, :, None] == jnp.arange(NBLK)[None, None, :]) & live_slots[:, :, None]
    return jnp.any(matches, axis=1)

def rounded(values):
    return lax.optimization_barrier(values.astype(jnp.bfloat16)).astype(jnp.float32)

def sample_back(inputs, incoming_sensitivity, block_list, live_count, layer_gains):
    gain_heads = layer_gains.reshape(4, HEADS, HEAD_DIM)
    norm_val, inv_rms = normed_of(inputs)
    queries = rounded(norm_val * gain_heads[0])
    key_mat = rounded(norm_val * gain_heads[1])
    val_mat = rounded(norm_val * gain_heads[2])
    scaling = HEAD_DIM ** (-0.5)
    scores = jnp.einsum('thd,shd->hts', queries, key_mat) * scaling
    permitted = allowed_blocks(block_list, live_count)
    token_mask = jnp.repeat(jnp.repeat(permitted, BLK, axis=0), BLK, axis=1)
    scores = jnp.where(token_mask[None], scores, -jnp.inf)
    exped = jnp.exp(scores - lax.optimization_barrier(jnp.max(scores, axis=-1, keepdims=True)))
    probs = exped / lax.optimization_barrier(jnp.sum(exped, axis=-1, keepdims=True))
    probs_low = rounded(probs)
    output = jnp.einsum('hts,shd->thd', probs_low, val_mat)
    incoming = incoming_sensitivity.astype(jnp.float32).reshape(SEQUENCE_SPAN, HEADS, HEAD_DIM)
    grad_out = rounded(gain_heads[3] * incoming)
    grad_probs = jnp.einsum('thd,shd->hts', grad_out, val_mat)
    grad_scores = rounded(probs * (grad_probs - lax.optimization_barrier(jnp.sum(probs * grad_probs, axis=-1, keepdims=True))))
    grad_query = jnp.einsum('hts,shd->thd', grad_scores, key_mat) * scaling
    scores_split = grad_scores.reshape(HEADS, N_SEQ, ROWS, SEQUENCE_SPAN)
    probs_split = probs_low.reshape(HEADS, N_SEQ, ROWS, SEQUENCE_SPAN)
    key_by = jnp.einsum('hqts,qthd->qshd', scores_split, queries.reshape(N_SEQ, ROWS, HEADS, HEAD_DIM)) * scaling
    value_by = jnp.einsum('hqts,qthd->qshd', probs_split, grad_out.reshape(N_SEQ, ROWS, HEADS, HEAD_DIM))
    grad_key = lax.optimization_barrier(jnp.sum(key_by, axis=0))
    grad_value = lax.optimization_barrier(jnp.sum(value_by, axis=0))
    grad_terms = jnp.stack([lax.optimization_barrier(jnp.sum(grad_query * norm_val, axis=0)), lax.optimization_barrier(jnp.sum(grad_key * norm_val, axis=0)), lax.optimization_barrier(jnp.sum(grad_value * norm_val, axis=0)), lax.optimization_barrier(jnp.sum(output * incoming, axis=0))])
    key_part = key_by * gain_heads[1] + value_by * gain_heads[2]
    same_half = (jnp.arange(N_SEQ)[:, None] == (jnp.arange(SEQUENCE_SPAN) // ROWS)[None, :])[:, :, None, None]
    self_part = lax.optimization_barrier(jnp.sum(jnp.where(same_half, key_part, 0.0), axis=0))
    cross_sum = lax.optimization_barrier(jnp.sum(jnp.where(same_half, 0.0, key_part), axis=0))
    cross_part = rounded(norm_back(cross_sum, norm_val, inv_rms))
    grad_input = incoming + norm_back(grad_query * gain_heads[0] + self_part, norm_val, inv_rms) + cross_part
    return (grad_input.reshape(SEQUENCE_SPAN, FEATURE_WIDTH), grad_terms.reshape(4, FEATURE_WIDTH))

def reference(stored_part_activation, pending_sensitivity, uppermost_result_derivative, scaling_factors, attended_tile_table, active_tile_number):

    def flatten(values):
        return values.reshape((WINDOW * MINIBATCH_SIZE,) + values.shape[2:])

    def depth_reverse_sweep(arriving_above, layer_items):
        x_layer, first_grad, layer_gains, ids_layer, count_layer = layer_items
        incoming_sensitivity = jnp.concatenate([first_grad.astype(jnp.float32)[None], arriving_above], axis=0)

        def one_sample(sample_items):
            return sample_back(sample_items[0], sample_items[1], sample_items[2], sample_items[3], layer_gains)
        grad_input, grad_terms = lax.map(one_sample, (flatten(x_layer), flatten(incoming_sensitivity), flatten(ids_layer), flatten(count_layer)))
        grad_input = grad_input.reshape(WINDOW, MINIBATCH_SIZE, SEQUENCE_SPAN, FEATURE_WIDTH)
        return (grad_input[:WINDOW - 1], lax.optimization_barrier(jnp.sum(grad_terms, axis=0)))
    starting_sensitivity = uppermost_result_derivative.astype(jnp.float32)
    final_sensitivity, factor_derivatives = lax.scan(depth_reverse_sweep, starting_sensitivity, (stored_part_activation, pending_sensitivity, scaling_factors, attended_tile_table, active_tile_number), reverse=True)
    return factor_derivatives
```

```python
import functools
import math

import jax
import jax.numpy as jnp
from jax import lax
from jax.experimental import pallas as pl
from jax.experimental.pallas import tpu as pltpu
from jax.sharding import PartitionSpec as P

HEAD_DIM = 128
BLK = 128
epsilon = 1e-06
MESH = pl.DeviceIdType.MESH
SCALE = HEAD_DIM ** (-0.5)
LOG2E = math.log2(math.e)
MASKED = -1e30

NT = (((1,), (1,)), ((), ()))
NN = (((1,), (0,)), ((), ()))
TN = (((0,), (0,)), ((), ()))


def mm(a, b, dims):
    return lax.dot_general(a, b, dims, preferred_element_type=jnp.float32)


def head_math(x, arr, gains, bias, with_input):
    g_query, g_key, g_val, gate = gains
    rows = x.shape[0]
    half = rows // 2
    xf = x.astype(jnp.float32)
    inv = lax.rsqrt(jnp.sum(xf * xf, axis=-1, keepdims=True) * (1.0 / HEAD_DIM) + epsilon)
    norm = xf * inv
    norm_low = norm.astype(jnp.bfloat16)
    qk = g_query * g_key
    vg = gate * g_val
    query = (norm * (qk * (SCALE * LOG2E))).astype(jnp.bfloat16)
    val = (norm * vg).astype(jnp.bfloat16)
    scores = mm(norm_low, query, NT)
    grad_probs = mm(val, arr, NT)
    lane = lax.broadcasted_iota(jnp.int32, (1, rows), 1)
    first = lane < half
    row_bias = [jnp.where(first, bias[c][0], bias[c][1]) for c in range(2)]
    parts = [scores[:half], scores[half:]]
    tops = [jnp.max(p, axis=0, keepdims=True) + b for p, b in zip(parts, row_bias)]
    top = jnp.maximum(tops[0], tops[1])
    exped = jnp.concatenate([jnp.exp2(p + (b - top)) for p, b in zip(parts, row_bias)], axis=0)
    probs = exped * (1.0 / jnp.sum(exped, axis=0, keepdims=True))
    weighted = probs * grad_probs
    grad_scores = weighted - probs * jnp.sum(weighted, axis=0, keepdims=True)
    ds = grad_scores.astype(jnp.bfloat16)
    back_val = mm(probs.astype(jnp.bfloat16), arr, NN)
    back_key = mm(ds, norm_low, NN)
    key_sum = jnp.sum(norm * back_key, axis=0, keepdims=True) * SCALE
    val_sum = jnp.sum(norm * back_val, axis=0, keepdims=True)
    if not with_input:
        return key_sum, val_sum, None
    back_query = mm(ds, norm_low, TN)
    u = (qk * SCALE) * (back_key + back_query) + vg * back_val
    centred = u - norm * (jnp.sum(u * norm, axis=-1, keepdims=True) * (1.0 / HEAD_DIM))
    grad_input = arr.astype(jnp.float32) + inv * centred
    return key_sum, val_sum, grad_input.astype(jnp.bfloat16)


def sweep_kernel(
    segments, n_dp, heads,
    x_ref, p_ref, u_ref, sf_ref, tab_ref, cnt_ref, out_ref,
    x_own, p_own, x_far, p_far, arr, gin, sfv, gath,
    lsem, x_s, x_r, p_s, p_r, arr_s, arr_r, red_s, red_r,
):
    seg = lax.axis_index("segment")
    dp = lax.axis_index("dp")
    seq = lax.axis_index("seq")
    far = {"seq": 1 - seq}
    below = {"segment": jnp.maximum(seg - 1, 0)}
    above = {"segment": jnp.minimum(seg + 1, segments - 1)}
    mine = pl.multiple_of(seq * (heads * HEAD_DIM), heads * HEAD_DIM)
    is_top = seg == segments - 1

    def group(d, s):
        return {"dp": lax.rem(dp + d, n_dp), "seq": lax.rem(seq + s, 2)}

    others = [(d, s) for s in range(2) for d in range(n_dp) if d + s > 0]

    width = heads * HEAD_DIM
    local = [
        pltpu.make_async_copy(x_ref.at[0, 0, 0, :, pl.ds(mine, width)], x_own.at[0], lsem.at[0]),
        pltpu.make_async_copy(p_ref.at[0, 0, :, pl.ds(mine, width)], p_own, lsem.at[1]),
        pltpu.make_async_copy(sf_ref.at[0], sfv, lsem.at[2]),
        pltpu.make_async_copy(x_ref.at[0, 1, 0, :, pl.ds(mine, width)], x_own.at[1], lsem.at[3]),
    ]
    for c in local:
        c.start()

    barrier = pltpu.get_barrier_semaphore()
    for d, s in others:
        pl.semaphore_signal(barrier, inc=1, device_id=group(d, s), device_id_type=MESH)

    @pl.when(seg > 0)
    def _():
        pl.semaphore_signal(barrier, inc=1, device_id=below, device_id_type=MESH)

    @pl.when(seg < segments - 1)
    def _():
        pl.semaphore_signal(barrier, inc=1, device_id=above, device_id_type=MESH)

    inner = jnp.where(seg > 0, 1, 0) + jnp.where(seg < segments - 1, 1, 0)
    pl.semaphore_wait(barrier, len(others) + inner)

    def far_cols(h):
        return pl.ds(pl.multiple_of(((1 - seq) * heads + h) * HEAD_DIM, HEAD_DIM), HEAD_DIM)

    def send_x(w, h):
        return pltpu.make_async_remote_copy(
            src_ref=x_ref.at[0, w, 0, :, far_cols(h)], dst_ref=x_far.at[w, h],
            send_sem=x_s.at[w, h], recv_sem=x_r.at[w, h], device_id=far, device_id_type=MESH,
        )

    def send_p(h):
        return pltpu.make_async_remote_copy(
            src_ref=p_ref.at[0, 0, :, far_cols(h)], dst_ref=p_far.at[h],
            send_sem=p_s.at[h], recv_sem=p_r.at[h], device_id=far, device_id_type=MESH,
        )

    def send_u(h):
        return pltpu.make_async_remote_copy(
            src_ref=u_ref.at[0, 0, :, far_cols(h)], dst_ref=arr.at[h, pl.ds(BLK, BLK)],
            send_sem=arr_s.at[h], recv_sem=arr_r.at[h], device_id=far, device_id_type=MESH,
        )

    def own_u(h):
        cols = pl.ds(pl.multiple_of(mine + h * HEAD_DIM, HEAD_DIM), HEAD_DIM)
        return pltpu.make_async_copy(
            u_ref.at[0, 0, :, cols], arr.at[h, pl.ds(0, BLK)], lsem.at[4 + h]
        )

    def send_down(h):
        return pltpu.make_async_remote_copy(
            src_ref=gin.at[h], dst_ref=arr.at[h],
            send_sem=p_s.at[heads + h], recv_sem=p_r.at[heads + h],
            device_id=below, device_id_type=MESH,
        )

    for h in range(2):
        send_x(0, h).start()
        send_p(h).start()

    def bias_of(w):
        rows = []
        for c in range(2):
            key_block = lax.rem(c + seq, 2)
            row = []
            for r in range(2):
                a = lax.rem(r + seq, 2)
                hit = (tab_ref[0, w, 0, a, 0] == key_block) | (
                    (cnt_ref[0, w, 0, a] > 1) & (tab_ref[0, w, 0, a, 1] == key_block)
                )
                row.append(jnp.where(hit, 0.0, MASKED).astype(jnp.float32))
            rows.append(row)
        return rows

    def gains_of(h):
        cols = pl.ds(pl.multiple_of(mine + h * HEAD_DIM, HEAD_DIM), HEAD_DIM)
        return [sfv[i : i + 1, cols] for i in range(4)]

    def head_cols(h):
        return pl.ds(pl.multiple_of(h * HEAD_DIM, HEAD_DIM), HEAD_DIM)

    slot = seq * n_dp + dp
    bias0 = bias_of(0)
    bias1 = bias_of(1)
    for c in local[:3]:
        c.wait()

    def first_batch(h, carry):
        send_x(0, h).wait_send()
        send_p(h).wait_send()

        @pl.when(h + 2 < heads)
        def _():
            send_x(0, h + 2).start()
            send_p(h + 2).start()

        @pl.when(h + 2 >= heads)
        def _():
            first = (h + 2 - heads) * 2
            send_x(1, first).start()
            send_x(1, first + 1).start()

        @pl.when(is_top)
        def _():
            own_u(h).start()
            send_u(h).start()

        send_x(0, h).wait_recv()
        send_p(h).wait_recv()
        x = jnp.concatenate([x_own[0, :, head_cols(h)], x_far[0, h]], axis=0)
        pend = jnp.concatenate([p_own[:, head_cols(h)], p_far[h]], axis=0)
        key_sum, val_sum, grad_input = head_math(x, pend, gains_of(h), bias0, True)
        gin[h] = grad_input

        @pl.when(seg > 0)
        def _():
            send_down(h).start()

        gath[slot, pl.ds(h, 1)] = key_sum
        gath[slot, pl.ds(heads + h, 1)] = val_sum
        return carry

    lax.fori_loop(0, heads, first_batch, 0)
    local[3].wait()

    def second_batch(h, carry):
        send_x(1, h).wait_send()

        @pl.when(h + 4 < heads)
        def _():
            send_x(1, h + 4).start()

        send_x(1, h).wait_recv()

        @pl.when(is_top)
        def _():
            own_u(h).wait()
            send_u(h).wait()

        @pl.when(seg < segments - 1)
        def _():
            send_down(h).wait_recv()

        x = jnp.concatenate([x_own[1, :, head_cols(h)], x_far[1, h]], axis=0)
        key_sum, val_sum, _ = head_math(x, arr[h], gains_of(h), bias1, False)
        gath[slot, pl.ds(h, 1)] += key_sum
        gath[slot, pl.ds(heads + h, 1)] += val_sum
        return carry

    lax.fori_loop(0, heads, second_batch, 0)

    shares = []
    for d, s in others:
        c = pltpu.make_async_remote_copy(
            src_ref=gath.at[slot], dst_ref=gath.at[slot],
            send_sem=red_s.at[s * n_dp + d], recv_sem=red_r.at[s * n_dp + d],
            device_id=group(d, s), device_id_type=MESH,
        )
        c.start()
        shares.append(c)

    @pl.when(seg > 0)
    def _():
        def drain(h, carry):
            send_down(h).wait_send()
            return carry

        lax.fori_loop(0, heads, drain, 0)

    for c in shares:
        c.wait()
    for s in range(2):
        total = gath[s * n_dp]
        for d in range(1, n_dp):
            total = total + gath[s * n_dp + d]
        for h in range(heads):
            cols = slice((s * heads + h) * HEAD_DIM, (s * heads + h + 1) * HEAD_DIM)
            key_sum = total[h : h + 1]
            val_sum = total[heads + h : heads + h + 1]
            out_ref[0, 0:1, cols] = sfv[1:2, cols] * key_sum
            out_ref[0, 1:2, cols] = sfv[0:1, cols] * key_sum
            out_ref[0, 2:3, cols] = sfv[3:4, cols] * val_sum
            out_ref[0, 3:4, cols] = sfv[2:3, cols] * val_sum


def shards(segments, n_dp, x, pend, top, gains, table, count):
    rows, channels = x.shape[3], x.shape[4]
    heads = channels // HEAD_DIM // 2
    width = heads * HEAD_DIM
    any_space = pl.BlockSpec(memory_space=pltpu.HBM)
    smem = pl.BlockSpec(memory_space=pltpu.SMEM)
    dma = pltpu.SemaphoreType.DMA
    low = jnp.bfloat16
    return pl.pallas_call(
        functools.partial(sweep_kernel, segments, n_dp, heads),
        out_shape=jax.ShapeDtypeStruct((1, 4, channels), jnp.float32),
        in_specs=[any_space] * 4 + [smem] * 2,
        out_specs=pl.BlockSpec(memory_space=pltpu.VMEM),
        scratch_shapes=[
            pltpu.VMEM((2, rows, width), low),
            pltpu.VMEM((rows, width), low),
            pltpu.VMEM((2, heads, rows, HEAD_DIM), low),
            pltpu.VMEM((heads, rows, HEAD_DIM), low),
            pltpu.VMEM((heads, 2 * rows, HEAD_DIM), low),
            pltpu.VMEM((heads, 2 * rows, HEAD_DIM), low),
            pltpu.VMEM((4, channels), jnp.float32),
            pltpu.VMEM((2 * n_dp, 2 * heads, HEAD_DIM), jnp.float32),
            dma((4 + heads,)),
            dma((2, heads)),
            dma((2, heads)),
            dma((2 * heads,)),
            dma((2 * heads,)),
            dma((heads,)),
            dma((heads,)),
            dma((2 * n_dp,)),
            dma((2 * n_dp,)),
        ],
        compiler_params=pltpu.CompilerParams(
            collective_id=1, has_side_effects=True, vmem_limit_bytes=48 << 20
        ),
        name="sweep",
    )(x, pend, top, gains, table, count)


def solution(mesh):
    placed = (
        P("segment", None, "dp", "seq", None),
        P("segment", "dp", "seq", None),
        P(None, "dp", "seq", None),
        P("segment", None, None),
        P("segment", None, "dp", None, None),
        P("segment", None, "dp", None),
    )
    body = functools.partial(shards, mesh.shape["segment"], mesh.shape["dp"])
    return jax.shard_map(
        body, mesh=mesh, in_specs=placed, out_specs=P("segment", None, None), check_vma=False
    )
```

```python
import functools
import math

import jax
import jax.numpy as jnp
from jax import lax
from jax.experimental import pallas as pl
from jax.experimental.pallas import tpu as pltpu
from jax.sharding import PartitionSpec as P

HEAD_DIM = 128
BLK = 128
epsilon = 1e-06
MESH = pl.DeviceIdType.MESH
SCALE = HEAD_DIM ** (-0.5)
LOG2E = math.log2(math.e)
MASKED = -1e30
RUN = 8
HELPERS = 3
LENDERS = 4

NT = (((1,), (1,)), ((), ()))
NN = (((1,), (0,)), ((), ()))
TN = (((0,), (0,)), ((), ()))


def mm(a, b, dims):
    return lax.dot_general(a, b, dims, preferred_element_type=jnp.float32)


def head_math(x, arr, gains, bias, with_input):
    g_query, g_key, g_val, gate = gains
    rows = x.shape[0]
    half = rows // 2
    xf = x.astype(jnp.float32)
    inv = lax.rsqrt(jnp.sum(xf * xf, axis=-1, keepdims=True) * (1.0 / HEAD_DIM) + epsilon)
    norm = xf * inv
    norm_low = norm.astype(jnp.bfloat16)
    qk = g_query * g_key
    vg = gate * g_val
    query = (norm * (qk * (SCALE * LOG2E))).astype(jnp.bfloat16)
    val = (norm * vg).astype(jnp.bfloat16)
    scores = mm(norm_low, query, NT)
    grad_probs = mm(val, arr, NT)
    lane = lax.broadcasted_iota(jnp.int32, (1, rows), 1)
    first = lane < half
    row_bias = [jnp.where(first, bias[c][0], bias[c][1]) for c in range(2)]
    parts = [scores[:half], scores[half:]]
    tops = [jnp.max(p, axis=0, keepdims=True) + b for p, b in zip(parts, row_bias)]
    top = jnp.maximum(tops[0], tops[1])
    exped = jnp.concatenate([jnp.exp2(p + (b - top)) for p, b in zip(parts, row_bias)], axis=0)
    probs = exped * (1.0 / jnp.sum(exped, axis=0, keepdims=True))
    weighted = probs * grad_probs
    grad_scores = weighted - probs * jnp.sum(weighted, axis=0, keepdims=True)
    ds = grad_scores.astype(jnp.bfloat16)
    back_val = mm(probs.astype(jnp.bfloat16), arr, NN)
    back_key = mm(ds, norm_low, NN)
    key_sum = jnp.sum(norm * back_key, axis=0, keepdims=True) * SCALE
    val_sum = jnp.sum(norm * back_val, axis=0, keepdims=True)
    if not with_input:
        return key_sum, val_sum, None
    back_query = mm(ds, norm_low, TN)
    u = (qk * SCALE) * (back_key + back_query) + vg * back_val
    centred = u - norm * (jnp.sum(u * norm, axis=-1, keepdims=True) * (1.0 / HEAD_DIM))
    grad_input = arr.astype(jnp.float32) + inv * centred
    return key_sum, val_sum, grad_input.astype(jnp.bfloat16)


def sweep_kernel(
    segments, n_dp, heads,
    x_ref, p_ref, u_ref, sf_ref, tab_ref, cnt_ref, out_ref,
    x_own, p_own, x_far, p_far, arr, gin, passing, sfv, gath,
    lsem, x_s, x_r, p_s, p_r, down_s, down_r, u_s, pass_s, pass_r, red_s, red_r, ready,
):
    seg = lax.axis_index("segment")
    dp = lax.axis_index("dp")
    seq = lax.axis_index("seq")
    z = lax.rem(seg, RUN)
    run = seg // RUN
    rank = seq * n_dp + dp
    far_rank = (1 - seq) * n_dp + dp
    far = {"seq": 1 - seq}
    mine = pl.multiple_of(seq * (heads * HEAD_DIM), heads * HEAD_DIM)

    is_top = seg == segments - 1
    edge_src = (z == 0) & (run > 0)
    edge_dst = (z == RUN - 1) & (seg < segments - 1)
    helper = (z > 0) & (z <= HELPERS) & (run > 0)
    plain_src = z > 0
    plain_dst = z < RUN - 1
    lender = (seg >= RUN - LENDERS) & (seg < RUN)
    borne = 2 * HELPERS
    lent = heads // LENDERS

    def at(section):
        return {"segment": section}

    def peer(t):
        return {"dp": lax.rem(t, n_dp), "seq": t // n_dp}

    def signal(sem, device):
        pl.semaphore_signal(sem, inc=1, device_id=device, device_id_type=MESH)

    barrier = pltpu.get_barrier_semaphore()
    signal(barrier, far)
    width = heads * HEAD_DIM
    local = [
        pltpu.make_async_copy(sf_ref.at[0], sfv, lsem.at[2]),
        pltpu.make_async_copy(x_ref.at[0, 0, 0, :, pl.ds(mine, width)], x_own.at[0], lsem.at[3]),
        pltpu.make_async_copy(p_ref.at[0, 0, :, pl.ds(mine, width)], p_own, lsem.at[4]),
        pltpu.make_async_copy(x_ref.at[0, 1, 0, :, pl.ds(mine, width)], x_own.at[1], lsem.at[5]),
    ]
    for c in local:
        c.start()

    @pl.when(plain_dst)
    def _():
        signal(barrier, at(seg + 1))

    @pl.when(edge_src)
    def _():
        signal(barrier, at(seg - 1))
        for k in range(1, HELPERS + 1):
            signal(barrier, at(seg + k))

    @pl.when(helper)
    def _():
        signal(barrier, at(seg - z - 1))

    @pl.when(lender)
    def _():
        signal(barrier, {"segment": segments - 1, "seq": 1 - seq})

    def greet(t, carry):
        @pl.when(t != far_rank)
        def _():
            signal(barrier, peer(t))

        return carry

    lax.fori_loop(rank + 1, 2 * n_dp, greet, 0)

    def one(cond, amount=1):
        return jnp.where(cond, amount, 0)

    earlier = rank - seq
    pl.semaphore_wait(
        barrier,
        1 + earlier + one(plain_src) + one(edge_dst, 1 + HELPERS) + one(helper) + one(is_top, LENDERS),
    )

    def far_cols(h):
        return pl.ds(pl.multiple_of(((1 - seq) * heads + h) * HEAD_DIM, HEAD_DIM), HEAD_DIM)

    def send_x(w, h):
        return pltpu.make_async_remote_copy(
            src_ref=x_ref.at[0, w, 0, :, far_cols(h)], dst_ref=x_far.at[w, h],
            send_sem=x_s.at[w, h], recv_sem=x_r.at[w, h], device_id=far, device_id_type=MESH,
        )

    def send_p(h):
        return pltpu.make_async_remote_copy(
            src_ref=p_ref.at[0, 0, :, far_cols(h)], dst_ref=p_far.at[h],
            send_sem=p_s.at[h], recv_sem=p_r.at[h], device_id=far, device_id_type=MESH,
        )

    def send_u(h):
        return pltpu.make_async_remote_copy(
            src_ref=u_ref.at[0, 0, :, far_cols(h)], dst_ref=arr.at[h, pl.ds(BLK, BLK)],
            send_sem=u_s.at[h], recv_sem=down_r.at[h],
            device_id={"segment": segments - 1, "seq": 1 - seq}, device_id_type=MESH,
        )

    def own_u(h):
        cols = pl.ds(pl.multiple_of(mine + h * HEAD_DIM, HEAD_DIM), HEAD_DIM)
        return pltpu.make_async_copy(
            u_ref.at[0, 0, :, cols], arr.at[h, pl.ds(0, BLK)], lsem.at[6 + h]
        )

    def send_down(h):
        return pltpu.make_async_remote_copy(
            src_ref=gin.at[h], dst_ref=arr.at[h],
            send_sem=down_s.at[h], recv_sem=down_r.at[h],
            device_id=at(lax.rem(seg + segments - 1, segments)), device_id_type=MESH,
        )

    def send_helper(h):
        return pltpu.make_async_remote_copy(
            src_ref=gin.at[h], dst_ref=passing.at[lax.rem(h, 2)],
            send_sem=down_s.at[h], recv_sem=pass_r.at[lax.rem(h, 2)],
            device_id=at(seg + 1 + h // 2), device_id_type=MESH,
        )

    def send_on(j):
        h = 2 * (z - 1) + j
        return pltpu.make_async_remote_copy(
            src_ref=passing.at[j], dst_ref=arr.at[h],
            send_sem=pass_s.at[j], recv_sem=down_r.at[h],
            device_id=at(seg - z - 1), device_id_type=MESH,
        )

    for h in range(2):
        send_x(0, h).start()
        send_p(h).start()

    @pl.when(edge_dst)
    def _():
        for k in range(HELPERS + 1):
            signal(ready.at[0], at(seg + 1 + k))

    @pl.when(helper)
    def _():
        signal(ready.at[1], at(seg - z))

    @pl.when(is_top)
    def _():
        for k in range(LENDERS):
            signal(ready.at[2], {"segment": RUN - 1 - k, "seq": 1 - seq})

    def answer(t, carry):
        @pl.when(t != far_rank)
        def _():
            signal(ready.at[3], peer(t))

        return carry

    lax.fori_loop(0, rank, answer, 0)

    def bias_of(w):
        rows = []
        for c in range(2):
            key_block = lax.rem(c + seq, 2)
            row = []
            for r in range(2):
                a = lax.rem(r + seq, 2)
                hit = (tab_ref[0, w, 0, a, 0] == key_block) | (
                    (cnt_ref[0, w, 0, a] > 1) & (tab_ref[0, w, 0, a, 1] == key_block)
                )
                row.append(jnp.where(hit, 0.0, MASKED).astype(jnp.float32))
            rows.append(row)
        return rows

    def gains_of(h):
        cols = pl.ds(pl.multiple_of(mine + h * HEAD_DIM, HEAD_DIM), HEAD_DIM)
        return [sfv[i : i + 1, cols] for i in range(4)]

    def head_cols(h):
        return pl.ds(pl.multiple_of(h * HEAD_DIM, HEAD_DIM), HEAD_DIM)

    for c in local[:3]:
        c.wait()
    bias0 = bias_of(0)
    bias1 = bias_of(1)

    @pl.when(edge_src)
    def _():
        pl.semaphore_wait(ready.at[0], 1)
        pl.semaphore_wait(ready.at[1], HELPERS)

    @pl.when(helper)
    def _():
        pl.semaphore_wait(ready.at[0], 1)

    @pl.when(lender)
    def _():
        pl.semaphore_wait(ready.at[2], 1)

    def first_batch(h, carry):
        send_x(0, h).wait_send()
        send_p(h).wait_send()

        @pl.when(h + 2 < heads)
        def _():
            send_x(0, h + 2).start()
            send_p(h + 2).start()

        @pl.when(h + 2 >= heads)
        def _():
            first = (h + 2 - heads) * 2
            send_x(1, first).start()
            send_x(1, first + 1).start()

        @pl.when(is_top)
        def _():
            own_u(h).start()

        @pl.when(lender & (h // lent == RUN - 1 - seg))
        def _():
            send_u(h).start()

        send_x(0, h).wait_recv()
        send_p(h).wait_recv()
        x = jnp.concatenate([x_own[0, :, head_cols(h)], x_far[0, h]], axis=0)
        pend = jnp.concatenate([p_own[:, head_cols(h)], p_far[h]], axis=0)
        key_sum, val_sum, grad_input = head_math(x, pend, gains_of(h), bias0, True)
        gin[h] = grad_input

        @pl.when(plain_src | (edge_src & (h >= borne)))
        def _():
            send_down(h).start()

        @pl.when(edge_src & (h < borne))
        def _():
            send_helper(h).start()

        @pl.when(helper & (h // 2 == z))
        def _():
            send_helper(h).wait_recv()
            send_on(lax.rem(h, 2)).start()

        gath[rank, pl.ds(h, 1)] = key_sum
        gath[rank, pl.ds(heads + h, 1)] = val_sum
        return carry

    lax.fori_loop(0, heads, first_batch, 0)
    local[3].wait()

    def second_batch(h, carry):
        send_x(1, h).wait_send()

        @pl.when(h + 4 < heads)
        def _():
            send_x(1, h + 4).start()

        send_x(1, h).wait_recv()

        @pl.when(is_top)
        def _():
            own_u(h).wait()
            send_u(h).wait_recv()

        @pl.when(seg < segments - 1)
        def _():
            send_down(h).wait_recv()

        x = jnp.concatenate([x_own[1, :, head_cols(h)], x_far[1, h]], axis=0)
        key_sum, val_sum, _ = head_math(x, arr[h], gains_of(h), bias1, False)
        gath[rank, pl.ds(h, 1)] += key_sum
        gath[rank, pl.ds(heads + h, 1)] += val_sum
        return carry

    lax.fori_loop(0, heads, second_batch, 0)

    later = 2 * n_dp - 1 - rank - (1 - seq)

    @pl.when(later > 0)
    def _():
        pl.semaphore_wait(ready.at[3], later)

    shares = []
    for d in range(1, 2 * n_dp):
        to = lax.rem(rank + d, 2 * n_dp)
        c = pltpu.make_async_remote_copy(
            src_ref=gath.at[rank], dst_ref=gath.at[rank],
            send_sem=red_s.at[d], recv_sem=red_r.at[d], device_id=peer(to), device_id_type=MESH,
        )
        c.start()
        shares.append(c)

    def drain_down(h, carry):
        @pl.when(plain_src | edge_src)
        def _():
            send_down(h).wait_send()

        @pl.when(lender & (h // lent == RUN - 1 - seg))
        def _():
            send_u(h).wait_send()

        return carry

    lax.fori_loop(0, heads, drain_down, 0)

    @pl.when(helper)
    def _():
        for j in range(2):
            send_on(j).wait_send()

    for c in shares:
        c.wait()
    for s in range(2):
        total = gath[s * n_dp]
        for d in range(1, n_dp):
            total = total + gath[s * n_dp + d]
        for h in range(heads):
            cols = slice((s * heads + h) * HEAD_DIM, (s * heads + h + 1) * HEAD_DIM)
            key_sum = total[h : h + 1]
            val_sum = total[heads + h : heads + h + 1]
            out_ref[0, 0:1, cols] = sfv[1:2, cols] * key_sum
            out_ref[0, 1:2, cols] = sfv[0:1, cols] * key_sum
            out_ref[0, 2:3, cols] = sfv[3:4, cols] * val_sum
            out_ref[0, 3:4, cols] = sfv[2:3, cols] * val_sum


def shards(segments, n_dp, x, pend, top, gains, table, count):
    rows, channels = x.shape[3], x.shape[4]
    heads = channels // HEAD_DIM // 2
    width = heads * HEAD_DIM
    in_place = pl.BlockSpec(memory_space=pltpu.HBM)
    dma = pltpu.SemaphoreType.DMA
    low = jnp.bfloat16
    return pl.pallas_call(
        functools.partial(sweep_kernel, segments, n_dp, heads),
        out_shape=jax.ShapeDtypeStruct((1, 4, channels), jnp.float32),
        in_specs=[in_place] * 4 + [pl.BlockSpec(memory_space=pltpu.SMEM)] * 2,
        out_specs=pl.BlockSpec(memory_space=pltpu.VMEM),
        scratch_shapes=[
            pltpu.VMEM((2, rows, width), low),
            pltpu.VMEM((rows, width), low),
            pltpu.VMEM((2, heads, rows, HEAD_DIM), low),
            pltpu.VMEM((heads, rows, HEAD_DIM), low),
            pltpu.VMEM((heads, 2 * rows, HEAD_DIM), low),
            pltpu.VMEM((heads, 2 * rows, HEAD_DIM), low),
            pltpu.VMEM((2, 2 * rows, HEAD_DIM), low),
            pltpu.VMEM((4, channels), jnp.float32),
            pltpu.VMEM((2 * n_dp, 2 * heads, HEAD_DIM), jnp.float32),
            dma((6 + heads,)),
            dma((2, heads)),
            dma((2, heads)),
            dma((heads,)),
            dma((heads,)),
            dma((heads,)),
            dma((heads,)),
            dma((heads,)),
            dma((2,)),
            dma((2,)),
            dma((2 * n_dp,)),
            dma((2 * n_dp,)),
            pltpu.SemaphoreType.REGULAR((4,)),
        ],
        compiler_params=pltpu.CompilerParams(
            collective_id=1, has_side_effects=True, vmem_limit_bytes=60 << 20
        ),
        name="sweep",
    )(x, pend, top, gains, table, count)


def solution(mesh):
    placed = (
        P("segment", None, "dp", "seq", None),
        P("segment", "dp", "seq", None),
        P(None, "dp", "seq", None),
        P("segment", None, None),
        P("segment", None, "dp", None, None),
        P("segment", None, "dp", None),
    )
    body = functools.partial(shards, mesh.shape["segment"], mesh.shape["dp"])
    return jax.shard_map(
        body, mesh=mesh, in_specs=placed, out_specs=P("segment", None, None), check_vma=False
    )
```

```python
import functools
import math

import jax
import jax.numpy as jnp
from jax import lax
from jax.experimental import pallas as pl
from jax.experimental.pallas import tpu as pltpu
from jax.sharding import PartitionSpec as P

HEAD_DIM = 128
BLK = 128
epsilon = 1e-06
MESH = pl.DeviceIdType.MESH
SCALE = HEAD_DIM ** (-0.5)
LOG2E = math.log2(math.e)
MASKED = -1e30
RUN = 8
HELPERS = 7
LENDERS = 8

NT = (((1,), (1,)), ((), ()))
NN = (((1,), (0,)), ((), ()))
TN = (((0,), (0,)), ((), ()))


def mm(a, b, dims):
    return lax.dot_general(a, b, dims, preferred_element_type=jnp.float32)


def head_math(x, arr, gains, bias, with_input):
    g_query, g_key, g_val, gate = gains
    rows = x.shape[0]
    half = rows // 2
    xf = x.astype(jnp.float32)
    inv = lax.rsqrt(jnp.sum(xf * xf, axis=-1, keepdims=True) * (1.0 / HEAD_DIM) + epsilon)
    norm = xf * inv
    norm_low = norm.astype(jnp.bfloat16)
    qk = g_query * g_key
    vg = gate * g_val
    query = (norm * (qk * (SCALE * LOG2E))).astype(jnp.bfloat16)
    val = (norm * vg).astype(jnp.bfloat16)
    scores = mm(norm_low, query, NT)
    grad_probs = mm(val, arr, NT)
    lane = lax.broadcasted_iota(jnp.int32, (1, rows), 1)
    first = lane < half
    row_bias = [jnp.where(first, bias[c][0], bias[c][1]) for c in range(2)]
    parts = [scores[:half], scores[half:]]
    tops = [jnp.max(p, axis=0, keepdims=True) + b for p, b in zip(parts, row_bias)]
    top = jnp.maximum(tops[0], tops[1])
    exped = jnp.concatenate([jnp.exp2(p + (b - top)) for p, b in zip(parts, row_bias)], axis=0)
    probs = exped * (1.0 / jnp.sum(exped, axis=0, keepdims=True))
    weighted = probs * grad_probs
    grad_scores = weighted - probs * jnp.sum(weighted, axis=0, keepdims=True)
    ds = grad_scores.astype(jnp.bfloat16)
    back_val = mm(probs.astype(jnp.bfloat16), arr, NN)
    back_key = mm(ds, norm_low, NN)
    key_sum = jnp.sum(norm * back_key, axis=0, keepdims=True) * SCALE
    val_sum = jnp.sum(norm * back_val, axis=0, keepdims=True)
    if not with_input:
        return key_sum, val_sum, None
    back_query = mm(ds, norm_low, TN)
    u = (qk * SCALE) * (back_key + back_query) + vg * back_val
    centred = u - norm * (jnp.sum(u * norm, axis=-1, keepdims=True) * (1.0 / HEAD_DIM))
    grad_input = arr.astype(jnp.float32) + inv * centred
    return key_sum, val_sum, grad_input.astype(jnp.bfloat16)


def sweep_kernel(
    segments, n_dp, heads,
    x_ref, p_ref, u_ref, sf_ref, tab_ref, cnt_ref, out_ref,
    x_own, p_own, x_far, p_far, arr, gin, passing, sfv, part, coll, mid, gath, table, count,
    lsem, x_s, x_r, p_s, p_r, down_s, down_r, u_s, pass_s, pass_r, one_s, one_r, two_s, two_r, red_s, red_r, ready,
):
    seg = lax.axis_index("segment")
    dp = lax.axis_index("dp")
    seq = lax.axis_index("seq")
    z = lax.rem(seg, RUN)
    run = seg // RUN
    rank = seq * n_dp + dp
    far_rank = (1 - seq) * n_dp + dp
    far = {"seq": 1 - seq}
    mine = pl.multiple_of(seq * (heads * HEAD_DIM), heads * HEAD_DIM)

    is_top = seg == segments - 1
    edge_src = (z == 0) & (run > 0)
    edge_dst = (z == RUN - 1) & (seg < segments - 1)
    helper = (z > 0) & (z <= HELPERS) & (run > 0)
    plain_src = z > 0
    plain_dst = z < RUN - 1
    lender = (seg >= RUN - LENDERS) & (seg < RUN)
    borne = HELPERS
    early = heads // 2
    lent = heads // LENDERS

    def at(section):
        return {"segment": section}

    def peer(t):
        return {"dp": lax.rem(t, n_dp), "seq": t // n_dp}

    def signal(sem, device):
        pl.semaphore_signal(sem, inc=1, device_id=device, device_id_type=MESH)

    barrier = pltpu.get_barrier_semaphore()
    signal(barrier, far)
    width = heads * HEAD_DIM
    local = [
        pltpu.make_async_copy(tab_ref.at[0, :, 0], table, lsem.at[0]),
        pltpu.make_async_copy(cnt_ref.at[0, :, 0], count, lsem.at[1]),
        pltpu.make_async_copy(sf_ref.at[0], sfv, lsem.at[2]),
        pltpu.make_async_copy(x_ref.at[0, 0, 0, :, pl.ds(mine, width)], x_own.at[0], lsem.at[3]),
        pltpu.make_async_copy(p_ref.at[0, 0, :, pl.ds(mine, width)], p_own, lsem.at[4]),
        pltpu.make_async_copy(x_ref.at[0, 1, 0, :, pl.ds(mine, width)], x_own.at[1], lsem.at[5]),
    ]
    for c in local:
        c.start()

    @pl.when(plain_dst)
    def _():
        signal(barrier, at(seg + 1))

    @pl.when(edge_src)
    def _():
        signal(barrier, at(seg - 1))
        for k in range(1, HELPERS + 1):
            signal(barrier, at(seg + k))

    @pl.when(helper)
    def _():
        signal(barrier, at(seg - z - 1))

    @pl.when(lender)
    def _():
        signal(barrier, {"segment": segments - 1, "seq": 1 - seq})

    def greet(t, carry):
        @pl.when(t != far_rank)
        def _():
            signal(barrier, peer(t))

        return carry

    lax.fori_loop(rank + 1, 2 * n_dp, greet, 0)

    def one(cond, amount=1):
        return jnp.where(cond, amount, 0)

    earlier = rank - seq
    pl.semaphore_wait(
        barrier,
        1 + earlier + one(plain_src) + one(edge_dst, 1 + HELPERS) + one(helper) + one(is_top, LENDERS),
    )

    def far_cols(h):
        return pl.ds(pl.multiple_of(((1 - seq) * heads + h) * HEAD_DIM, HEAD_DIM), HEAD_DIM)

    def send_x(w, h):
        return pltpu.make_async_remote_copy(
            src_ref=x_ref.at[0, w, 0, :, far_cols(h)], dst_ref=x_far.at[w, h],
            send_sem=x_s.at[w, h], recv_sem=x_r.at[w, h], device_id=far, device_id_type=MESH,
        )

    def send_p(h):
        return pltpu.make_async_remote_copy(
            src_ref=p_ref.at[0, 0, :, far_cols(h)], dst_ref=p_far.at[h],
            send_sem=p_s.at[h], recv_sem=p_r.at[h], device_id=far, device_id_type=MESH,
        )

    def send_u(h):
        return pltpu.make_async_remote_copy(
            src_ref=u_ref.at[0, 0, :, far_cols(h)], dst_ref=arr.at[h, pl.ds(BLK, BLK)],
            send_sem=u_s.at[h], recv_sem=down_r.at[h],
            device_id={"segment": segments - 1, "seq": 1 - seq}, device_id_type=MESH,
        )

    def own_u(h):
        cols = pl.ds(pl.multiple_of(mine + h * HEAD_DIM, HEAD_DIM), HEAD_DIM)
        return pltpu.make_async_copy(
            u_ref.at[0, 0, :, cols], arr.at[h, pl.ds(0, BLK)], lsem.at[6 + h]
        )

    def send_down(h):
        return pltpu.make_async_remote_copy(
            src_ref=gin.at[h], dst_ref=arr.at[h],
            send_sem=down_s.at[h], recv_sem=down_r.at[h],
            device_id=at(lax.rem(seg + segments - 1, segments)), device_id_type=MESH,
        )

    def send_helper(h):
        return pltpu.make_async_remote_copy(
            src_ref=gin.at[h], dst_ref=passing,
            send_sem=down_s.at[h], recv_sem=pass_r.at[0],
            device_id=at(lax.rem(seg + 1 + h, segments)), device_id_type=MESH,
        )

    def send_on():
        return pltpu.make_async_remote_copy(
            src_ref=passing, dst_ref=arr.at[z - 1],
            send_sem=pass_s.at[0], recv_sem=down_r.at[z - 1],
            device_id=at(seg - z - 1), device_id_type=MESH,
        )

    for h in range(2):
        send_x(0, h).start()
        send_p(h).start()

    @pl.when(edge_dst)
    def _():
        for k in range(HELPERS + 1):
            signal(ready.at[0], at(seg + 1 + k))

    @pl.when(helper)
    def _():
        signal(ready.at[2 + z], at(seg - z))

    @pl.when(is_top)
    def _():
        for k in range(LENDERS):
            signal(ready.at[1], {"segment": RUN - 1 - k, "seq": 1 - seq})

    def answer(t, carry):
        @pl.when(t != far_rank)
        def _():
            signal(ready.at[2], peer(t))

        return carry

    lax.fori_loop(0, rank, answer, 0)

    def bias_of(w):
        rows = []
        for c in range(2):
            key_block = lax.rem(c + seq, 2)
            row = []
            for r in range(2):
                a = lax.rem(r + seq, 2)
                hit = (table[w, a, 0] == key_block) | (
                    (count[w, a] > 1) & (table[w, a, 1] == key_block)
                )
                row.append(jnp.where(hit, 0.0, MASKED).astype(jnp.float32))
            rows.append(row)
        return rows

    def gains_of(h):
        cols = pl.ds(pl.multiple_of(mine + h * HEAD_DIM, HEAD_DIM), HEAD_DIM)
        return [sfv[i : i + 1, cols] for i in range(4)]

    def head_cols(h):
        return pl.ds(pl.multiple_of(h * HEAD_DIM, HEAD_DIM), HEAD_DIM)

    for c in local[:5]:
        c.wait()
    bias0 = bias_of(0)
    bias1 = bias_of(1)

    def first_batch(h, carry):
        send_x(0, h).wait_send()
        send_p(h).wait_send()

        @pl.when(h + 2 < heads)
        def _():
            send_x(0, h + 2).start()
            send_p(h + 2).start()

        @pl.when(h + 2 >= heads)
        def _():
            first = (h + 2 - heads) * 2
            send_x(1, first).start()
            send_x(1, first + 1).start()

        @pl.when(is_top)
        def _():
            own_u(h).start()

        @pl.when(lender & (h // lent == RUN - 1 - seg))
        def _():
            pl.semaphore_wait(ready.at[1], 1)
            send_u(h).start()

        send_x(0, h).wait_recv()
        send_p(h).wait_recv()
        x = jnp.concatenate([x_own[0, :, head_cols(h)], x_far[0, h]], axis=0)
        pend = jnp.concatenate([p_own[:, head_cols(h)], p_far[h]], axis=0)
        key_sum, val_sum, grad_input = head_math(x, pend, gains_of(h), bias0, True)
        gin[h] = grad_input

        @pl.when(edge_src & (h == borne))
        def _():
            pl.semaphore_wait(ready.at[0], 1)

        @pl.when(plain_src | (edge_src & (h >= borne)))
        def _():
            send_down(h).start()

        @pl.when(edge_src & (h < borne))
        def _():
            pl.semaphore_wait(ready.at[3 + h], 1)
            send_helper(h).start()

        @pl.when(helper & (h == z))
        def _():
            pl.semaphore_wait(ready.at[0], 1)
            send_helper(h - 1).wait_recv()
            send_on().start()

        @pl.when(h < early)
        def _():
            part[h] = key_sum
            part[early + h] = val_sum

        @pl.when(h >= early)
        def _():
            gath[rank, pl.ds(h - early, 1)] = key_sum
            gath[rank, pl.ds(h, 1)] = val_sum

        return carry

    lax.fori_loop(0, heads, first_batch, 0)
    local[5].wait()

    later = 2 * n_dp - 1 - rank - (1 - seq)

    def send_part(d):
        to = lax.rem(dp + d, n_dp)
        return pltpu.make_async_remote_copy(
            src_ref=part.at[to], dst_ref=coll.at[dp],
            send_sem=one_s.at[d], recv_sem=one_r.at[d], device_id={"dp": to}, device_id_type=MESH,
        )

    def send_mid(d):
        return pltpu.make_async_remote_copy(
            src_ref=mid.at[rank], dst_ref=mid.at[rank],
            send_sem=two_s.at[d], recv_sem=two_r.at[d],
            device_id=peer(lax.rem(rank + d, 2 * n_dp)), device_id_type=MESH,
        )

    def second_batch(h, carry):
        send_x(1, h).wait_send()

        @pl.when(h + 4 < heads)
        def _():
            send_x(1, h + 4).start()

        send_x(1, h).wait_recv()

        @pl.when(is_top)
        def _():
            own_u(h).wait()
            send_u(h).wait_recv()

        @pl.when(seg < segments - 1)
        def _():
            send_down(h).wait_recv()

        x = jnp.concatenate([x_own[1, :, head_cols(h)], x_far[1, h]], axis=0)
        key_sum, val_sum, _ = head_math(x, arr[h], gains_of(h), bias1, False)
        @pl.when(h < early)
        def _():
            part[h] += key_sum
            part[early + h] += val_sum

        @pl.when(h >= early)
        def _():
            gath[rank, pl.ds(h - early, 1)] += key_sum
            gath[rank, pl.ds(h, 1)] += val_sum

        @pl.when(h == early - 1)
        def _():
            @pl.when(later > 0)
            def _():
                pl.semaphore_wait(ready.at[2], later)

            coll[dp] = part[dp]
            for d in range(1, n_dp):
                send_part(d).start()

        @pl.when(h == heads - 2)
        def _():
            for d in range(1, n_dp):
                send_part(d).wait_recv()
            total = coll[0]
            for d in range(1, n_dp):
                total = total + coll[d]
            mid[rank] = total
            for d in range(1, 2 * n_dp):
                send_mid(d).start()

        return carry

    lax.fori_loop(0, heads, second_batch, 0)

    shares = []
    for d in range(1, 2 * n_dp):
        to = lax.rem(rank + d, 2 * n_dp)
        c = pltpu.make_async_remote_copy(
            src_ref=gath.at[rank], dst_ref=gath.at[rank],
            send_sem=red_s.at[d], recv_sem=red_r.at[d], device_id=peer(to), device_id_type=MESH,
        )
        c.start()
        shares.append(c)

    for d in range(1, 2 * n_dp):
        send_mid(d).wait_recv()
    for c in shares:
        c.wait_recv()
    for s in range(2):
        total = gath[s * n_dp]
        for d in range(1, n_dp):
            total = total + gath[s * n_dp + d]
        for h in range(heads):
            cols = slice((s * heads + h) * HEAD_DIM, (s * heads + h + 1) * HEAD_DIM)
            if h < early:
                key_sum = mid[s * n_dp + h]
                val_sum = mid[s * n_dp + early + h]
            else:
                key_sum = total[h - early : h - early + 1]
                val_sum = total[h : h + 1]
            out_ref[0, 0:1, cols] = sfv[1:2, cols] * key_sum
            out_ref[0, 1:2, cols] = sfv[0:1, cols] * key_sum
            out_ref[0, 2:3, cols] = sfv[3:4, cols] * val_sum
            out_ref[0, 3:4, cols] = sfv[2:3, cols] * val_sum

    def drain_down(h, carry):
        @pl.when(plain_src | edge_src)
        def _():
            send_down(h).wait_send()

        @pl.when(lender & (h // lent == RUN - 1 - seg))
        def _():
            send_u(h).wait_send()

        return carry

    lax.fori_loop(0, heads, drain_down, 0)

    @pl.when(helper)
    def _():
        send_on().wait_send()

    for d in range(1, n_dp):
        send_part(d).wait_send()
    for d in range(1, 2 * n_dp):
        send_mid(d).wait_send()
    for c in shares:
        c.wait_send()


def shards(segments, n_dp, x, pend, top, gains, table, count):
    rows, channels = x.shape[3], x.shape[4]
    heads = channels // HEAD_DIM // 2
    width = heads * HEAD_DIM
    in_place = pl.BlockSpec(memory_space=pltpu.HBM)
    dma = pltpu.SemaphoreType.DMA
    low = jnp.bfloat16
    return pl.pallas_call(
        functools.partial(sweep_kernel, segments, n_dp, heads),
        out_shape=jax.ShapeDtypeStruct((1, 4, channels), jnp.float32),
        in_specs=[in_place] * 6,
        out_specs=pl.BlockSpec(memory_space=pltpu.VMEM),
        scratch_shapes=[
            pltpu.VMEM((2, rows, width), low),
            pltpu.VMEM((rows, width), low),
            pltpu.VMEM((2, heads, rows, HEAD_DIM), low),
            pltpu.VMEM((heads, rows, HEAD_DIM), low),
            pltpu.VMEM((heads, 2 * rows, HEAD_DIM), low),
            pltpu.VMEM((heads, 2 * rows, HEAD_DIM), low),
            pltpu.VMEM((2 * rows, HEAD_DIM), low),
            pltpu.VMEM((4, channels), jnp.float32),
            pltpu.VMEM((n_dp, 1, HEAD_DIM), jnp.float32),
            pltpu.VMEM((n_dp, 1, HEAD_DIM), jnp.float32),
            pltpu.VMEM((2 * n_dp, 1, HEAD_DIM), jnp.float32),
            pltpu.VMEM((2 * n_dp, heads, HEAD_DIM), jnp.float32),
            pltpu.SMEM((2, 2, 2), jnp.int32),
            pltpu.SMEM((2, 2), jnp.int32),
            dma((6 + heads,)),
            dma((2, heads)),
            dma((2, heads)),
            dma((heads,)),
            dma((heads,)),
            dma((heads,)),
            dma((heads,)),
            dma((heads,)),
            dma((1,)),
            dma((1,)),
            dma((n_dp,)),
            dma((n_dp,)),
            dma((2 * n_dp,)),
            dma((2 * n_dp,)),
            dma((2 * n_dp,)),
            dma((2 * n_dp,)),
            pltpu.SemaphoreType.REGULAR((3 + HELPERS,)),
        ],
        compiler_params=pltpu.CompilerParams(
            collective_id=1, has_side_effects=True, vmem_limit_bytes=32 << 20
        ),
        name="sweep",
    )(*[pltpu.with_memory_space_constraint(v, pltpu.HBM) for v in (x, pend, top, gains, table, count)])


def solution(mesh):
    placed = (
        P("segment", None, "dp", "seq", None),
        P("segment", "dp", "seq", None),
        P(None, "dp", "seq", None),
        P("segment", None, None),
        P("segment", None, "dp", None, None),
        P("segment", None, "dp", None),
    )
    body = functools.partial(shards, mesh.shape["segment"], mesh.shape["dp"])
    return jax.shard_map(
        body, mesh=mesh, in_specs=placed, out_specs=P("segment", None, None), check_vma=False
    )
```

```python
import functools
import math

import jax
import jax.numpy as jnp
from jax import lax
from jax.experimental import pallas as pl
from jax.experimental.pallas import tpu as pltpu
from jax.sharding import PartitionSpec as P

HEAD_DIM = 128
BLK = 128
epsilon = 1e-06
MESH = pl.DeviceIdType.MESH
SCALE = HEAD_DIM ** (-0.5)
LOG2E = math.log2(math.e)
MASKED = -1e30
RUN = 8
LOOK = 4
HELPERS = 7
LENDERS = 8

NT = (((1,), (1,)), ((), ()))
NN = (((1,), (0,)), ((), ()))
TN = (((0,), (0,)), ((), ()))


def mm(a, b, dims):
    return lax.dot_general(a, b, dims, preferred_element_type=jnp.float32)


def head_math(x, arr, qk, vg, row_bias, with_input):
    rows = x.shape[0]
    half = rows // 2
    xf = x.astype(jnp.float32)
    inv = lax.rsqrt(jnp.sum(xf * xf, axis=-1, keepdims=True) * (1.0 / HEAD_DIM) + epsilon)
    norm = xf * inv
    norm_low = norm.astype(jnp.bfloat16)
    query = (norm * (qk * (SCALE * LOG2E))).astype(jnp.bfloat16)
    val = (norm * vg).astype(jnp.bfloat16)
    scores = mm(norm_low, query, NT)
    grad_probs = mm(val, arr, NT)
    parts = [scores[:half], scores[half:]]
    tops = [jnp.max(p, axis=0, keepdims=True) + b for p, b in zip(parts, row_bias)]
    top = jnp.maximum(tops[0], tops[1])
    exped = jnp.concatenate([jnp.exp2(p + (b - top)) for p, b in zip(parts, row_bias)], axis=0)
    probs = exped * (1.0 / jnp.sum(exped, axis=0, keepdims=True))
    weighted = probs * grad_probs
    grad_scores = weighted - probs * jnp.sum(weighted, axis=0, keepdims=True)
    ds = grad_scores.astype(jnp.bfloat16)
    back_val = mm(probs.astype(jnp.bfloat16), arr, NN)
    back_key = mm(ds, norm_low, NN)
    key_sum = jnp.sum(norm * back_key, axis=0, keepdims=True) * SCALE
    val_sum = jnp.sum(norm * back_val, axis=0, keepdims=True)
    if not with_input:
        return key_sum, val_sum, None
    back_query = mm(ds, norm_low, TN)
    u = (qk * SCALE) * (back_key + back_query) + vg * back_val
    centred = u - norm * (jnp.sum(u * norm, axis=-1, keepdims=True) * (1.0 / HEAD_DIM))
    grad_input = arr.astype(jnp.float32) + inv * centred
    return key_sum, val_sum, grad_input.astype(jnp.bfloat16)


def sweep_kernel(
    segments, n_dp, heads,
    x_ref, p_ref, u_ref, sf_ref, tab_ref, cnt_ref, out_ref,
    x_in, p_in, arr, gin, passing, sfv, meta, meta_in, part, late, coll, tot, mid, gath, table, count,
    lsem, x_s, x_r, p_s, p_r, m_s, m_r, down_s, down_r, u_s, pass_s, pass_r,
    one_s, one_r, two_s, two_r, red_s, red_r, ready,
):
    seg = lax.axis_index("segment")
    dp = lax.axis_index("dp")
    seq = lax.axis_index("seq")
    z = lax.rem(seg, RUN)
    run = seg // RUN
    ring = 2 * (segments // RUN)
    y = seq * (ring // 2) + run
    reach = ring // 4

    def place(dy, zz=None, to_dp=None):
        yy = lax.rem(y + dy + 2 * ring, ring)
        where = {
            "segment": lax.rem(yy, ring // 2) * RUN + (z if zz is None else zz),
            "seq": yy // (ring // 2),
        }
        if to_dp is not None:
            where["dp"] = to_dp
        return where

    sides = (-reach, reach)
    work = lax.rem(seg + segments // 2, segments)
    work_run = work // RUN

    def heads_at(dy):
        return lax.rem(y + dy + reach + 2 * ring, ring) // (ring // 2)

    here = heads_at(0)
    seq_of_side = (1 - here, here)

    is_top = work == segments - 1
    edge_src = (z == 0) & (work_run > 0)
    edge_dst = (z == RUN - 1) & (work < segments - 1)
    helper = (z > 0) & (work_run > 0)
    plain_src = z > 0
    plain_dst = z < RUN - 1
    lender = run == segments // RUN - 1
    borne = HELPERS
    early = heads // 2

    def at(section):
        return {"segment": section}

    def signal(sem, device):
        pl.semaphore_signal(sem, inc=1, device_id=device, device_id_type=MESH)

    barrier = pltpu.get_barrier_semaphore()
    for dy in sides:
        signal(barrier, place(dy))
    local = [
        pltpu.make_async_copy(tab_ref.at[0, :, 0], table, lsem.at[0]),
        pltpu.make_async_copy(cnt_ref.at[0, :, 0], count, lsem.at[1]),
        pltpu.make_async_copy(sf_ref.at[0], sfv, lsem.at[2]),
    ]
    for c in local:
        c.start()

    @pl.when(plain_dst)
    def _():
        signal(barrier, at(seg + 1))

    @pl.when(edge_src)
    def _():
        signal(barrier, place(-1, RUN - 1))
        for k in range(1, HELPERS + 1):
            signal(barrier, at(lax.rem(seg + k, segments)))

    @pl.when(helper)
    def _():
        signal(barrier, place(-1, RUN - 1))

    top_at = {"segment": segments // 2 - 1, "seq": 1 - seq}

    @pl.when(lender)
    def _():
        signal(barrier, top_at)

    def greet(t, carry):
        signal(barrier, place(0, None, t))
        return carry

    lax.fori_loop(dp + 1, n_dp, greet, 0)
    higher = [lax.rem(y + dy + ring, ring) > y for dy in sides]
    for dy, up in zip(sides, higher):
        @pl.when(up)
        def _():
            for d in range(1, n_dp):
                signal(barrier, place(dy, None, lax.rem(dp + d, n_dp)))

    def one(cond, amount=1):
        return jnp.where(cond, amount, 0)

    pl.semaphore_wait(
        barrier,
        2 + dp + sum(one(~up, n_dp - 1) for up in higher) + one(plain_src)
        + one(edge_dst, 1 + HELPERS) + one(helper) + one(is_top, LENDERS),
    )

    def cols_of(group, h):
        return pl.ds(pl.multiple_of((group * heads + h) * HEAD_DIM, HEAD_DIM), HEAD_DIM)

    def send_x(w, k, h):
        dy = (reach, -reach)[k]
        return pltpu.make_async_remote_copy(
            src_ref=x_ref.at[0, w, 0, :, cols_of(heads_at(dy), h)], dst_ref=x_in.at[w, k, h],
            send_sem=x_s.at[w, k, h], recv_sem=x_r.at[w, k, h],
            device_id=place(dy), device_id_type=MESH,
        )

    def send_p(k, h):
        dy = (reach, -reach)[k]
        return pltpu.make_async_remote_copy(
            src_ref=p_ref.at[0, 0, :, cols_of(heads_at(dy), h)], dst_ref=p_in.at[k, h],
            send_sem=p_s.at[k, h], recv_sem=p_r.at[k, h],
            device_id=place(dy), device_id_type=MESH,
        )

    def send_meta():
        return pltpu.make_async_remote_copy(
            src_ref=meta, dst_ref=meta_in, send_sem=m_s.at[0], recv_sem=m_r.at[0],
            device_id=place(reach), device_id_type=MESH,
        )

    def send_u(h):
        return pltpu.make_async_remote_copy(
            src_ref=u_ref.at[0, 0, :, cols_of(1 - seq, h)], dst_ref=arr.at[h, pl.ds(0, BLK)],
            send_sem=u_s.at[h], recv_sem=down_r.at[h], device_id=top_at, device_id_type=MESH,
        )

    def own_u(h):
        return pltpu.make_async_copy(
            u_ref.at[0, 0, :, cols_of(here, h)], arr.at[h, pl.ds(BLK, BLK)], lsem.at[3 + h]
        )

    def send_down(h):
        return pltpu.make_async_remote_copy(
            src_ref=gin.at[h], dst_ref=arr.at[h],
            send_sem=down_s.at[h], recv_sem=down_r.at[h],
            device_id=at(lax.rem(seg + segments - 1, segments)), device_id_type=MESH,
        )

    def send_edge(h):
        return pltpu.make_async_remote_copy(
            src_ref=gin.at[h], dst_ref=arr.at[h],
            send_sem=down_s.at[h], recv_sem=down_r.at[h],
            device_id=place(-1, RUN - 1), device_id_type=MESH,
        )

    def send_helper(h):
        return pltpu.make_async_remote_copy(
            src_ref=gin.at[h], dst_ref=passing,
            send_sem=down_s.at[h], recv_sem=pass_r.at[0],
            device_id=at(lax.rem(seg + 1 + h, segments)), device_id_type=MESH,
        )

    def send_on():
        return pltpu.make_async_remote_copy(
            src_ref=passing, dst_ref=arr.at[z - 1],
            send_sem=pass_s.at[0], recv_sem=down_r.at[z - 1],
            device_id=place(-1, RUN - 1), device_id_type=MESH,
        )

    for h in range(LOOK):
        for k in range(2):
            send_x(0, k, h).start()
            send_p(k, h).start()

    for c in local:
        c.wait()
    ahead = heads_at(reach)
    for h in range(heads):
        cols = cols_of(ahead, h)
        meta[h : h + 1] = sfv[0:1, cols] * sfv[1:2, cols]
        meta[heads + h : heads + h + 1] = sfv[3:4, cols] * sfv[2:3, cols]
    for w in range(2):
        for c in range(2):
            for a in range(2):
                hit = (table[w, a, 0] == c) | ((count[w, a] > 1) & (table[w, a, 1] == c))
                row = 2 * heads + 4 * w + 2 * c + a
                value = jnp.where(hit, 0.0, MASKED).astype(jnp.float32)
                meta[row : row + 1] = jnp.full((1, HEAD_DIM), value, jnp.float32)
    send_meta().start()

    @pl.when(edge_dst)
    def _():
        for k in range(HELPERS + 1):
            signal(ready.at[0], place(1, k))

    @pl.when(helper)
    def _():
        signal(ready.at[2 + z], at(seg - z))

    @pl.when(is_top)
    def _():
        for k in range(LENDERS):
            signal(ready.at[1], {"segment": segments - RUN + k, "seq": 1 - seq})

    def answer(t, carry):
        signal(ready.at[2], place(0, None, t))
        return carry

    lax.fori_loop(0, dp, answer, 0)
    for dy, up in zip(sides, higher):
        @pl.when(~up)
        def _():
            for d in range(1, n_dp):
                signal(ready.at[2], place(dy, None, lax.rem(dp + d, n_dp)))

    later = n_dp - 1 - dp + sum(one(up, n_dp - 1) for up in higher)

    def bias_of(w):
        rows = []
        for c in range(2):
            base = 2 * heads + 4 * w + 2 * seq_of_side[c]
            rows.append(
                jnp.concatenate(
                    [meta_in[pl.ds(base + seq_of_side[r], 1)] for r in range(2)], axis=1
                )
            )
        return rows

    def first_batch(h, carry):
        for k in range(2):
            send_x(0, k, h).wait_send()
            send_p(k, h).wait_send()

            @pl.when(h + LOOK < heads)
            def _():
                send_x(0, k, h + LOOK).start()
                send_p(k, h + LOOK).start()

            @pl.when(h + LOOK >= heads)
            def _():
                first = (h + LOOK - heads) * 2
                send_x(1, k, first).start()
                send_x(1, k, first + 1).start()

        @pl.when(is_top)
        def _():
            own_u(h).start()

        @pl.when(lender & (h == heads - 1 - z))
        def _():
            pl.semaphore_wait(ready.at[1], 1)
            send_u(h).start()

        @pl.when(h == 0)
        def _():
            send_meta().wait_recv()

        for k in range(2):
            send_x(0, k, h).wait_recv()
            send_p(k, h).wait_recv()
        x = jnp.concatenate([x_in[0, 0, h], x_in[0, 1, h]], axis=0)
        pend = jnp.concatenate([p_in[0, h], p_in[1, h]], axis=0)
        key_sum, val_sum, grad_input = head_math(
            x, pend, meta_in[pl.ds(h, 1)], meta_in[pl.ds(heads + h, 1)], bias_of(0), True
        )
        gin[h] = grad_input

        @pl.when(plain_src)
        def _():
            send_down(h).start()

        @pl.when(edge_src & (h < borne))
        def _():
            pl.semaphore_wait(ready.at[3 + h], 1)
            send_helper(h).start()

        @pl.when(edge_src & (h == borne))
        def _():
            pl.semaphore_wait(ready.at[0], 1)
            send_edge(h).start()

        @pl.when(helper & (h == jnp.minimum(jnp.maximum(z + 1, 3), heads - 1)))
        def _():
            pl.semaphore_wait(ready.at[0], 1)
            send_helper(z - 1).wait_recv()
            send_on().start()

        @pl.when(h < early)
        def _():
            part[h] = key_sum
            part[early + h] = val_sum

        @pl.when(h >= early)
        def _():
            late[pl.ds(h - early, 1)] = key_sum
            late[pl.ds(h, 1)] = val_sum

        return carry

    lax.fori_loop(0, heads, first_batch, 0)

    def send_part(d):
        to = lax.rem(dp + d, n_dp)
        return pltpu.make_async_remote_copy(
            src_ref=part.at[to], dst_ref=coll.at[dp],
            send_sem=one_s.at[d], recv_sem=one_r.at[d], device_id={"dp": to}, device_id_type=MESH,
        )

    def send_mid(k, d):
        return pltpu.make_async_remote_copy(
            src_ref=tot, dst_ref=mid.at[here, dp],
            send_sem=two_s.at[k, d], recv_sem=two_r.at[k, d],
            device_id=place(sides[k], None, lax.rem(dp + d, n_dp)), device_id_type=MESH,
        )

    def send_late(k, d):
        return pltpu.make_async_remote_copy(
            src_ref=late, dst_ref=gath.at[here, dp],
            send_sem=red_s.at[k, d], recv_sem=red_r.at[k, d],
            device_id=place(sides[k], None, lax.rem(dp + d, n_dp)), device_id_type=MESH,
        )

    order = [(k, d) for d in (4, 3, 5, 2, 6, 1, 7, 0) for k in range(2)]

    def second_batch(h, carry):
        for k in range(2):
            send_x(1, k, h).wait_send()

            @pl.when(h + 2 * LOOK < heads)
            def _():
                send_x(1, k, h + 2 * LOOK).start()

        for k in range(2):
            send_x(1, k, h).wait_recv()

        @pl.when(is_top)
        def _():
            own_u(h).wait()
            send_u(h).wait_recv()

        @pl.when(work < segments - 1)
        def _():
            send_down(h).wait_recv()

        x = jnp.concatenate([x_in[1, 0, h], x_in[1, 1, h]], axis=0)
        key_sum, val_sum, _ = head_math(
            x, arr[h], meta_in[pl.ds(h, 1)], meta_in[pl.ds(heads + h, 1)], bias_of(1), False
        )

        @pl.when(h < early)
        def _():
            part[h] += key_sum
            part[early + h] += val_sum

        @pl.when(h >= early)
        def _():
            late[pl.ds(h - early, 1)] += key_sum
            late[pl.ds(h, 1)] += val_sum

        @pl.when(h == early - 1)
        def _():
            @pl.when(later > 0)
            def _():
                pl.semaphore_wait(ready.at[2], later)

            coll[dp] = part[dp]
            for d in range(1, n_dp):
                send_part(d).start()

        @pl.when(h == heads - 2)
        def _():
            for d in range(1, n_dp):
                send_part(d).wait_recv()
            total = coll[0]
            for d in range(1, n_dp):
                total = total + coll[d]
            tot[...] = total
            for k, d in order:
                send_mid(k, d).start()

        return carry

    lax.fori_loop(0, heads, second_batch, 0)

    for k, d in order:
        send_late(k, d).start()
    for k, d in order:
        send_mid(k, d).wait_recv()
    for k, d in order:
        send_late(k, d).wait_recv()
    for s in range(2):
        total = gath[s, 0]
        for d in range(1, n_dp):
            total = total + gath[s, d]
        for h in range(heads):
            cols = slice((s * heads + h) * HEAD_DIM, (s * heads + h + 1) * HEAD_DIM)
            if h < early:
                key_sum = mid[s, h]
                val_sum = mid[s, early + h]
            else:
                key_sum = total[h - early : h - early + 1]
                val_sum = total[h : h + 1]
            out_ref[0, 0:1, cols] = sfv[1:2, cols] * key_sum
            out_ref[0, 1:2, cols] = sfv[0:1, cols] * key_sum
            out_ref[0, 2:3, cols] = sfv[3:4, cols] * val_sum
            out_ref[0, 3:4, cols] = sfv[2:3, cols] * val_sum

    def drain_down(h, carry):
        @pl.when(plain_src | edge_src)
        def _():
            send_down(h).wait_send()

        @pl.when(lender & (h == heads - 1 - z))
        def _():
            send_u(h).wait_send()

        return carry

    lax.fori_loop(0, heads, drain_down, 0)

    @pl.when(helper)
    def _():
        send_on().wait_send()

    send_meta().wait_send()
    for d in range(1, n_dp):
        send_part(d).wait_send()
    for k, d in order:
        send_mid(k, d).wait_send()
        send_late(k, d).wait_send()


def shards(segments, n_dp, x, pend, top, gains, table, count):
    rows, channels = x.shape[3], x.shape[4]
    heads = channels // HEAD_DIM // 2
    in_place = pl.BlockSpec(memory_space=pltpu.HBM)
    dma = pltpu.SemaphoreType.DMA
    low = jnp.bfloat16
    return pl.pallas_call(
        functools.partial(sweep_kernel, segments, n_dp, heads),
        out_shape=jax.ShapeDtypeStruct((1, 4, channels), jnp.float32),
        in_specs=[in_place] * 6,
        out_specs=pl.BlockSpec(memory_space=pltpu.VMEM),
        scratch_shapes=[
            pltpu.VMEM((2, 2, heads, rows, HEAD_DIM), low),
            pltpu.VMEM((2, heads, rows, HEAD_DIM), low),
            pltpu.VMEM((heads, 2 * rows, HEAD_DIM), low),
            pltpu.VMEM((heads, 2 * rows, HEAD_DIM), low),
            pltpu.VMEM((2 * rows, HEAD_DIM), low),
            pltpu.VMEM((4, channels), jnp.float32),
            pltpu.VMEM((2 * heads + 8, HEAD_DIM), jnp.float32),
            pltpu.VMEM((2 * heads + 8, HEAD_DIM), jnp.float32),
            pltpu.VMEM((n_dp, 1, HEAD_DIM), jnp.float32),
            pltpu.VMEM((heads, HEAD_DIM), jnp.float32),
            pltpu.VMEM((n_dp, 1, HEAD_DIM), jnp.float32),
            pltpu.VMEM((1, HEAD_DIM), jnp.float32),
            pltpu.VMEM((2, n_dp, 1, HEAD_DIM), jnp.float32),
            pltpu.VMEM((2, n_dp, heads, HEAD_DIM), jnp.float32),
            pltpu.SMEM((2, 2, 2), jnp.int32),
            pltpu.SMEM((2, 2), jnp.int32),
            dma((3 + heads,)),
            dma((2, 2, heads)),
            dma((2, 2, heads)),
            dma((2, heads)),
            dma((2, heads)),
            dma((1,)),
            dma((1,)),
            dma((heads,)),
            dma((heads,)),
            dma((heads,)),
            dma((1,)),
            dma((1,)),
            dma((n_dp,)),
            dma((n_dp,)),
            dma((2, n_dp)),
            dma((2, n_dp)),
            dma((2, n_dp)),
            dma((2, n_dp)),
            pltpu.SemaphoreType.REGULAR((3 + HELPERS,)),
        ],
        compiler_params=pltpu.CompilerParams(
            collective_id=1, has_side_effects=True, vmem_limit_bytes=32 << 20
        ),
        name="sweep",
    )(*[pltpu.with_memory_space_constraint(v, pltpu.HBM) for v in (x, pend, top, gains, table, count)])


def solution(mesh):
    placed = (
        P("segment", None, "dp", "seq", None),
        P("segment", "dp", "seq", None),
        P(None, "dp", "seq", None),
        P("segment", None, None),
        P("segment", None, "dp", None, None),
        P("segment", None, "dp", None),
    )
    body = functools.partial(shards, mesh.shape["segment"], mesh.shape["dp"])
    return jax.shard_map(
        body, mesh=mesh, in_specs=placed, out_specs=P("segment", None, None), check_vma=False
    )
```

```python
import functools
import math

import jax
import jax.numpy as jnp
from jax import lax
from jax.experimental import pallas as pl
from jax.experimental.pallas import tpu as pltpu
from jax.sharding import PartitionSpec as P

HEAD_DIM = 128
BLK = 128
epsilon = 1e-06
MESH = pl.DeviceIdType.MESH
SCALE = HEAD_DIM ** (-0.5)
LOG2E = math.log2(math.e)
MASKED = -1e30
RUN = 8
LOOK = 4
HELPERS = 7
LENDERS = 8

NT = (((1,), (1,)), ((), ()))
NN = (((1,), (0,)), ((), ()))
TN = (((0,), (0,)), ((), ()))


def mm(a, b, dims):
    return lax.dot_general(a, b, dims, preferred_element_type=jnp.float32)


def head_math(x, arr, qk, vg, row_bias, with_input):
    rows = x.shape[0]
    half = rows // 2
    xf = x.astype(jnp.float32)
    inv = lax.rsqrt(jnp.sum(xf * xf, axis=-1, keepdims=True) * (1.0 / HEAD_DIM) + epsilon)
    norm = xf * inv
    norm_low = norm.astype(jnp.bfloat16)
    query = (norm * (qk * (SCALE * LOG2E))).astype(jnp.bfloat16)
    val = (norm * vg).astype(jnp.bfloat16)
    scores = mm(norm_low, query, NT)
    grad_probs = mm(val, arr, NT)
    parts = [scores[:half], scores[half:]]
    tops = [jnp.max(p, axis=0, keepdims=True) + b for p, b in zip(parts, row_bias)]
    top = jnp.maximum(tops[0], tops[1])
    exped = jnp.concatenate([jnp.exp2(p + (b - top)) for p, b in zip(parts, row_bias)], axis=0)
    probs = exped * (1.0 / jnp.sum(exped, axis=0, keepdims=True))
    weighted = probs * grad_probs
    grad_scores = weighted - probs * jnp.sum(weighted, axis=0, keepdims=True)
    ds = grad_scores.astype(jnp.bfloat16)
    back_val = mm(probs.astype(jnp.bfloat16), arr, NN)
    back_key = mm(ds, norm_low, NN)
    key_sum = jnp.sum(norm * back_key, axis=0, keepdims=True) * SCALE
    val_sum = jnp.sum(norm * back_val, axis=0, keepdims=True)
    if not with_input:
        return key_sum, val_sum, None
    back_query = mm(ds, norm_low, TN)
    u = (qk * SCALE) * (back_key + back_query) + vg * back_val
    centred = u - norm * (jnp.sum(u * norm, axis=-1, keepdims=True) * (1.0 / HEAD_DIM))
    grad_input = arr.astype(jnp.float32) + inv * centred
    return key_sum, val_sum, grad_input.astype(jnp.bfloat16)


def sweep_kernel(
    segments, n_dp, heads,
    x_ref, p_ref, u_ref, sf_ref, tab_ref, cnt_ref, out_ref,
    x_in, p_in, arr, gin, passing, sfv, meta, meta_in, part, late, coll, tot, mid, gath, table, count,
    lsem, x_s, x_r, p_s, p_r, m_s, m_r, down_s, down_r, u_s, pass_s, pass_r,
    one_s, one_r, two_s, two_r, red_s, red_r, ready,
):
    seg = lax.axis_index("segment")
    dp = lax.axis_index("dp")
    seq = lax.axis_index("seq")
    z = lax.rem(seg, RUN)
    run = seg // RUN
    ring = 2 * (segments // RUN)
    y = seq * (ring // 2) + run
    reach = ring // 4

    def place(dy, zz=None, to_dp=None):
        yy = lax.rem(y + dy + 2 * ring, ring)
        where = {
            "segment": lax.rem(yy, ring // 2) * RUN + (z if zz is None else zz),
            "seq": yy // (ring // 2),
        }
        if to_dp is not None:
            where["dp"] = to_dp
        return where

    sides = (-reach, reach)
    work = lax.rem(seg + segments // 2, segments)
    work_run = work // RUN

    def heads_at(dy):
        return lax.rem(y + dy + reach + 2 * ring, ring) // (ring // 2)

    here = heads_at(0)
    seq_of_side = (1 - here, here)

    is_top = work == segments - 1
    edge_src = (z == 0) & (work_run > 0)
    edge_dst = (z == RUN - 1) & (work < segments - 1)
    helper = (z > 0) & (work_run > 0)
    plain_src = z > 0
    plain_dst = z < RUN - 1
    lender = run == segments // RUN - 1
    borne = HELPERS
    early = heads // 2

    def at(section):
        return {"segment": section}

    def signal(sem, device):
        pl.semaphore_signal(sem, inc=1, device_id=device, device_id_type=MESH)

    barrier = pltpu.get_barrier_semaphore()
    for dy in sides:
        signal(barrier, place(dy))
    local = [
        pltpu.make_async_copy(tab_ref.at[0, :, 0], table, lsem.at[0]),
        pltpu.make_async_copy(cnt_ref.at[0, :, 0], count, lsem.at[1]),
        pltpu.make_async_copy(sf_ref.at[0], sfv, lsem.at[2]),
    ]
    for c in local:
        c.start()

    @pl.when(plain_dst)
    def _():
        signal(barrier, at(seg + 1))

    @pl.when(edge_src)
    def _():
        signal(barrier, place(-1, RUN - 1))
        for k in range(1, HELPERS + 1):
            signal(barrier, at(lax.rem(seg + k, segments)))

    @pl.when(helper)
    def _():
        signal(barrier, place(-1, RUN - 1))

    top_at = {"segment": segments // 2 - 1, "seq": 1 - seq}

    @pl.when(lender)
    def _():
        signal(barrier, top_at)

    back = jnp.where(z == 0, 1, 0)
    line = lax.rem(y + ring - back, ring)
    turn = lax.rem(dp + n_dp - back, n_dp)

    def greet(t, carry):
        signal(barrier, place(0, None, lax.rem(t + back, n_dp)))
        return carry

    lax.fori_loop(turn + 1, n_dp, greet, 0)
    higher = [lax.rem(line + dy + ring, ring) > line for dy in sides]
    for dy, up in zip(sides, higher):
        @pl.when(up)
        def _():
            for d in range(1, n_dp):
                signal(barrier, place(dy, None, lax.rem(dp + d, n_dp)))

    def one(cond, amount=1):
        return jnp.where(cond, amount, 0)

    pl.semaphore_wait(
        barrier,
        2 + turn + sum(one(~up, n_dp - 1) for up in higher) + one(plain_src)
        + one(edge_dst, 1 + HELPERS) + one(helper) + one(is_top, LENDERS),
    )

    def cols_of(group, h):
        return pl.ds(pl.multiple_of((group * heads + h) * HEAD_DIM, HEAD_DIM), HEAD_DIM)

    def send_x(w, k, h):
        dy = (reach, -reach)[k]
        return pltpu.make_async_remote_copy(
            src_ref=x_ref.at[0, w, 0, :, cols_of(heads_at(dy), h)], dst_ref=x_in.at[w, k, h],
            send_sem=x_s.at[w, k, h], recv_sem=x_r.at[w, k, h],
            device_id=place(dy), device_id_type=MESH,
        )

    def send_p(k, h):
        dy = (reach, -reach)[k]
        return pltpu.make_async_remote_copy(
            src_ref=p_ref.at[0, 0, :, cols_of(heads_at(dy), h)], dst_ref=p_in.at[k, h],
            send_sem=p_s.at[k, h], recv_sem=p_r.at[k, h],
            device_id=place(dy), device_id_type=MESH,
        )

    def send_meta():
        return pltpu.make_async_remote_copy(
            src_ref=meta, dst_ref=meta_in, send_sem=m_s.at[0], recv_sem=m_r.at[0],
            device_id=place(reach), device_id_type=MESH,
        )

    def send_u(h):
        return pltpu.make_async_remote_copy(
            src_ref=u_ref.at[0, 0, :, cols_of(1 - seq, h)], dst_ref=arr.at[h, pl.ds(0, BLK)],
            send_sem=u_s.at[h], recv_sem=down_r.at[h], device_id=top_at, device_id_type=MESH,
        )

    def own_u(h):
        return pltpu.make_async_copy(
            u_ref.at[0, 0, :, cols_of(here, h)], arr.at[h, pl.ds(BLK, BLK)], lsem.at[3 + h]
        )

    def send_down(h):
        return pltpu.make_async_remote_copy(
            src_ref=gin.at[h], dst_ref=arr.at[h],
            send_sem=down_s.at[h], recv_sem=down_r.at[h],
            device_id=at(lax.rem(seg + segments - 1, segments)), device_id_type=MESH,
        )

    def send_edge(h):
        return pltpu.make_async_remote_copy(
            src_ref=gin.at[h], dst_ref=arr.at[h],
            send_sem=down_s.at[h], recv_sem=down_r.at[h],
            device_id=place(-1, RUN - 1), device_id_type=MESH,
        )

    def send_helper(h):
        return pltpu.make_async_remote_copy(
            src_ref=gin.at[h], dst_ref=passing,
            send_sem=down_s.at[h], recv_sem=pass_r.at[0],
            device_id=at(lax.rem(seg + 1 + h, segments)), device_id_type=MESH,
        )

    def send_on():
        return pltpu.make_async_remote_copy(
            src_ref=passing, dst_ref=arr.at[z - 1],
            send_sem=pass_s.at[0], recv_sem=down_r.at[z - 1],
            device_id=place(-1, RUN - 1), device_id_type=MESH,
        )

    for h in range(LOOK):
        for k in range(2):
            send_x(0, k, h).start()
            send_p(k, h).start()

    for c in local:
        c.wait()
    ahead = heads_at(reach)
    for h in range(heads):
        cols = cols_of(ahead, h)
        meta[h : h + 1] = sfv[0:1, cols] * sfv[1:2, cols]
        meta[heads + h : heads + h + 1] = sfv[3:4, cols] * sfv[2:3, cols]
    for w in range(2):
        for c in range(2):
            for a in range(2):
                hit = (table[w, a, 0] == c) | ((count[w, a] > 1) & (table[w, a, 1] == c))
                row = 2 * heads + 4 * w + 2 * c + a
                value = jnp.where(hit, 0.0, MASKED).astype(jnp.float32)
                meta[row : row + 1] = jnp.full((1, HEAD_DIM), value, jnp.float32)
    send_meta().start()

    @pl.when(edge_dst)
    def _():
        for k in range(HELPERS + 1):
            signal(ready.at[0], place(1, k))

    @pl.when(helper)
    def _():
        signal(ready.at[2 + z], at(seg - z))

    @pl.when(is_top)
    def _():
        for k in range(LENDERS):
            signal(ready.at[1], {"segment": segments - RUN + k, "seq": 1 - seq})

    def answer(t, carry):
        signal(ready.at[2], place(0, None, lax.rem(t + back, n_dp)))
        return carry

    lax.fori_loop(0, turn, answer, 0)
    for dy, up in zip(sides, higher):
        @pl.when(~up)
        def _():
            for d in range(1, n_dp):
                signal(ready.at[2], place(dy, None, lax.rem(dp + d, n_dp)))

    later = n_dp - 1 - turn + sum(one(up, n_dp - 1) for up in higher)

    def bias_of(w):
        rows = []
        for c in range(2):
            base = 2 * heads + 4 * w + 2 * seq_of_side[c]
            rows.append(
                jnp.concatenate(
                    [meta_in[pl.ds(base + seq_of_side[r], 1)] for r in range(2)], axis=1
                )
            )
        return rows

    def first_batch(h, carry):
        for k in range(2):
            send_x(0, k, h).wait_send()
            send_p(k, h).wait_send()

            @pl.when(h + LOOK < heads)
            def _():
                send_x(0, k, h + LOOK).start()
                send_p(k, h + LOOK).start()

            @pl.when(h + LOOK >= heads)
            def _():
                first = (h + LOOK - heads) * 2
                send_x(1, k, first).start()
                send_x(1, k, first + 1).start()

        @pl.when(is_top)
        def _():
            own_u(h).start()

        @pl.when(lender & (h == heads - 1 - z))
        def _():
            pl.semaphore_wait(ready.at[1], 1)
            send_u(h).start()

        @pl.when(h == 0)
        def _():
            send_meta().wait_recv()

        for k in range(2):
            send_x(0, k, h).wait_recv()
            send_p(k, h).wait_recv()
        x = jnp.concatenate([x_in[0, 0, h], x_in[0, 1, h]], axis=0)
        pend = jnp.concatenate([p_in[0, h], p_in[1, h]], axis=0)
        key_sum, val_sum, grad_input = head_math(
            x, pend, meta_in[pl.ds(h, 1)], meta_in[pl.ds(heads + h, 1)], bias_of(0), True
        )
        gin[h] = grad_input

        @pl.when(plain_src)
        def _():
            send_down(h).start()

        @pl.when(edge_src & (h < borne))
        def _():
            pl.semaphore_wait(ready.at[3 + h], 1)
            send_helper(h).start()

        @pl.when(edge_src & (h == borne))
        def _():
            pl.semaphore_wait(ready.at[0], 1)
            send_edge(h).start()

        @pl.when(helper & (h == jnp.minimum(jnp.maximum(z + 1, 5), heads - 1)))
        def _():
            pl.semaphore_wait(ready.at[0], 1)
            send_helper(z - 1).wait_recv()
            send_on().start()

        @pl.when(h < early)
        def _():
            part[h] = key_sum
            part[early + h] = val_sum

        @pl.when(h >= early)
        def _():
            late[pl.ds(h - early, 1)] = key_sum
            late[pl.ds(h, 1)] = val_sum

        return carry

    lax.fori_loop(0, heads, first_batch, 0)

    def send_part(d):
        to = lax.rem(dp + d, n_dp)
        return pltpu.make_async_remote_copy(
            src_ref=part.at[to], dst_ref=coll.at[dp],
            send_sem=one_s.at[d], recv_sem=one_r.at[d], device_id={"dp": to}, device_id_type=MESH,
        )

    def send_mid(k, d):
        return pltpu.make_async_remote_copy(
            src_ref=tot, dst_ref=mid.at[here, dp],
            send_sem=two_s.at[k, d], recv_sem=two_r.at[k, d],
            device_id=place(sides[k], None, lax.rem(dp + d, n_dp)), device_id_type=MESH,
        )

    def send_late(k, d):
        return pltpu.make_async_remote_copy(
            src_ref=late, dst_ref=gath.at[here, dp],
            send_sem=red_s.at[k, d], recv_sem=red_r.at[k, d],
            device_id=place(sides[k], None, lax.rem(dp + d, n_dp)), device_id_type=MESH,
        )

    order = [(k, d) for d in (4, 3, 5, 2, 6, 1, 7, 0) for k in range(2)]

    def second_batch(h, carry):
        for k in range(2):
            send_x(1, k, h).wait_send()

            @pl.when(h + 2 * LOOK < heads)
            def _():
                send_x(1, k, h + 2 * LOOK).start()

        for k in range(2):
            send_x(1, k, h).wait_recv()

        @pl.when(is_top)
        def _():
            own_u(h).wait()
            send_u(h).wait_recv()

        @pl.when(work < segments - 1)
        def _():
            send_down(h).wait_recv()

        x = jnp.concatenate([x_in[1, 0, h], x_in[1, 1, h]], axis=0)
        key_sum, val_sum, _ = head_math(
            x, arr[h], meta_in[pl.ds(h, 1)], meta_in[pl.ds(heads + h, 1)], bias_of(1), False
        )

        @pl.when(h < early)
        def _():
            part[h] += key_sum
            part[early + h] += val_sum

        @pl.when(h >= early)
        def _():
            late[pl.ds(h - early, 1)] += key_sum
            late[pl.ds(h, 1)] += val_sum

        @pl.when(h == early - 1)
        def _():
            @pl.when(later > 0)
            def _():
                pl.semaphore_wait(ready.at[2], later)

            coll[dp] = part[dp]
            for d in range(1, n_dp):
                send_part(d).start()

        return carry

    lax.fori_loop(0, heads, second_batch, 0)

    for k, d in order:
        send_late(k, d).start()
    for d in range(1, n_dp):
        send_part(d).wait_recv()
    total = coll[0]
    for d in range(1, n_dp):
        total = total + coll[d]
    tot[...] = total
    for k, d in order:
        send_mid(k, d).start()
    def write(s, h, key_sum, val_sum):
        cols = slice((s * heads + h) * HEAD_DIM, (s * heads + h + 1) * HEAD_DIM)
        out_ref[0, 0:1, cols] = sfv[1:2, cols] * key_sum
        out_ref[0, 1:2, cols] = sfv[0:1, cols] * key_sum
        out_ref[0, 2:3, cols] = sfv[3:4, cols] * val_sum
        out_ref[0, 3:4, cols] = sfv[2:3, cols] * val_sum

    for k, d in order:
        send_late(k, d).wait_recv()
    for s in range(2):
        total = gath[s, 0]
        for d in range(1, n_dp):
            total = total + gath[s, d]
        for h in range(early, heads):
            write(s, h, total[h - early : h - early + 1], total[h : h + 1])
    for k, d in order:
        send_mid(k, d).wait_recv()
    for s in range(2):
        for h in range(early):
            write(s, h, mid[s, h], mid[s, early + h])

    def drain_down(h, carry):
        @pl.when(plain_src | edge_src)
        def _():
            send_down(h).wait_send()

        @pl.when(lender & (h == heads - 1 - z))
        def _():
            send_u(h).wait_send()

        return carry

    lax.fori_loop(0, heads, drain_down, 0)

    @pl.when(helper)
    def _():
        send_on().wait_send()

    send_meta().wait_send()
    for d in range(1, n_dp):
        send_part(d).wait_send()
    for k, d in order:
        send_mid(k, d).wait_send()
        send_late(k, d).wait_send()


def shards(segments, n_dp, x, pend, top, gains, table, count):
    rows, channels = x.shape[3], x.shape[4]
    heads = channels // HEAD_DIM // 2
    in_place = pl.BlockSpec(memory_space=pltpu.HBM)
    dma = pltpu.SemaphoreType.DMA
    low = jnp.bfloat16
    return pl.pallas_call(
        functools.partial(sweep_kernel, segments, n_dp, heads),
        out_shape=jax.ShapeDtypeStruct((1, 4, channels), jnp.float32),
        in_specs=[in_place] * 6,
        out_specs=pl.BlockSpec(memory_space=pltpu.VMEM),
        scratch_shapes=[
            pltpu.VMEM((2, 2, heads, rows, HEAD_DIM), low),
            pltpu.VMEM((2, heads, rows, HEAD_DIM), low),
            pltpu.VMEM((heads, 2 * rows, HEAD_DIM), low),
            pltpu.VMEM((heads, 2 * rows, HEAD_DIM), low),
            pltpu.VMEM((2 * rows, HEAD_DIM), low),
            pltpu.VMEM((4, channels), jnp.float32),
            pltpu.VMEM((2 * heads + 8, HEAD_DIM), jnp.float32),
            pltpu.VMEM((2 * heads + 8, HEAD_DIM), jnp.float32),
            pltpu.VMEM((n_dp, 1, HEAD_DIM), jnp.float32),
            pltpu.VMEM((heads, HEAD_DIM), jnp.float32),
            pltpu.VMEM((n_dp, 1, HEAD_DIM), jnp.float32),
            pltpu.VMEM((1, HEAD_DIM), jnp.float32),
            pltpu.VMEM((2, n_dp, 1, HEAD_DIM), jnp.float32),
            pltpu.VMEM((2, n_dp, heads, HEAD_DIM), jnp.float32),
            pltpu.SMEM((2, 2, 2), jnp.int32),
            pltpu.SMEM((2, 2), jnp.int32),
            dma((3 + heads,)),
            dma((2, 2, heads)),
            dma((2, 2, heads)),
            dma((2, heads)),
            dma((2, heads)),
            dma((1,)),
            dma((1,)),
            dma((heads,)),
            dma((heads,)),
            dma((heads,)),
            dma((1,)),
            dma((1,)),
            dma((n_dp,)),
            dma((n_dp,)),
            dma((2, n_dp)),
            dma((2, n_dp)),
            dma((2, n_dp)),
            dma((2, n_dp)),
            pltpu.SemaphoreType.REGULAR((3 + HELPERS,)),
        ],
        compiler_params=pltpu.CompilerParams(
            collective_id=1, has_side_effects=True, vmem_limit_bytes=32 << 20
        ),
        name="sweep",
    )(*[pltpu.with_memory_space_constraint(v, pltpu.HBM) for v in (x, pend, top, gains, table, count)])


def solution(mesh):
    placed = (
        P("segment", None, "dp", "seq", None),
        P("segment", "dp", "seq", None),
        P(None, "dp", "seq", None),
        P("segment", None, None),
        P("segment", None, "dp", None, None),
        P("segment", None, "dp", None),
    )
    body = functools.partial(shards, mesh.shape["segment"], mesh.shape["dp"])
    return jax.shard_map(
        body, mesh=mesh, in_specs=placed, out_specs=P("segment", None, None), check_vma=False
    )
```

```python
import functools
import math

import jax
import jax.numpy as jnp
from jax import lax
from jax.experimental import pallas as pl
from jax.experimental.pallas import tpu as pltpu
from jax.sharding import PartitionSpec as P

HEAD_DIM = 128
BLK = 128
epsilon = 1e-06
MESH = pl.DeviceIdType.MESH
SCALE = HEAD_DIM ** (-0.5)
LOG2E = math.log2(math.e)
MASKED = -1e30
RUN = 8
LOOK = 4
HELPERS = 7
LENDERS = 8

NT = (((1,), (1,)), ((), ()))
NN = (((1,), (0,)), ((), ()))
TN = (((0,), (0,)), ((), ()))


def mm(a, b, dims):
    return lax.dot_general(a, b, dims, preferred_element_type=jnp.float32)


def head_math(x, arr, qk, vg, row_bias, with_input):
    rows = x.shape[0]
    half = rows // 2
    xf = x.astype(jnp.float32)
    inv = lax.rsqrt(jnp.sum(xf * xf, axis=-1, keepdims=True) * (1.0 / HEAD_DIM) + epsilon)
    norm = xf * inv
    norm_low = norm.astype(jnp.bfloat16)
    query = (norm * (qk * (SCALE * LOG2E))).astype(jnp.bfloat16)
    val = (norm * vg).astype(jnp.bfloat16)
    scores = mm(norm_low, query, NT)
    grad_probs = mm(val, arr, NT)
    parts = [scores[:half], scores[half:]]
    tops = [jnp.max(p, axis=0, keepdims=True) + b for p, b in zip(parts, row_bias)]
    top = jnp.maximum(tops[0], tops[1])
    exped = jnp.concatenate([jnp.exp2(p + (b - top)) for p, b in zip(parts, row_bias)], axis=0)
    probs = exped * (1.0 / jnp.sum(exped, axis=0, keepdims=True))
    weighted = probs * grad_probs
    grad_scores = weighted - probs * jnp.sum(weighted, axis=0, keepdims=True)
    ds = grad_scores.astype(jnp.bfloat16)
    back_val = mm(probs.astype(jnp.bfloat16), arr, NN)
    back_key = mm(ds, norm_low, NN)
    key_sum = jnp.sum(norm * back_key, axis=0, keepdims=True) * SCALE
    val_sum = jnp.sum(norm * back_val, axis=0, keepdims=True)
    if not with_input:
        return key_sum, val_sum, None
    back_query = mm(ds, norm_low, TN)
    u = (qk * SCALE) * (back_key + back_query) + vg * back_val
    centred = u - norm * (jnp.sum(u * norm, axis=-1, keepdims=True) * (1.0 / HEAD_DIM))
    grad_input = arr.astype(jnp.float32) + inv * centred
    return key_sum, val_sum, grad_input.astype(jnp.bfloat16)


def sweep_kernel(
    segments, n_dp, heads,
    x_ref, p_ref, u_ref, sf_ref, tab_ref, cnt_ref, out_ref,
    x_in, p_in, arr, gin, passing, sfv, meta, meta_in, part, late, coll, tot, mid, gath, table, count,
    lsem, x_s, x_r, p_s, p_r, m_s, m_r, down_s, down_r, u_s, pass_s, pass_r,
    one_s, one_r, two_s, two_r, red_s, red_r, ready,
):
    seg = lax.axis_index("segment")
    dp = lax.axis_index("dp")
    seq = lax.axis_index("seq")
    z = lax.rem(seg, RUN)
    run = seg // RUN
    ring = 2 * (segments // RUN)
    y = seq * (ring // 2) + run
    reach = ring // 4

    def place(dy, zz=None, to_dp=None):
        yy = lax.rem(y + dy + 2 * ring, ring)
        where = {
            "segment": lax.rem(yy, ring // 2) * RUN + (z if zz is None else zz),
            "seq": yy // (ring // 2),
        }
        if to_dp is not None:
            where["dp"] = to_dp
        return where

    sides = (-reach, reach)
    work = lax.rem(seg + segments // 2, segments)
    work_run = work // RUN

    def heads_at(dy):
        return lax.rem(y + dy + reach + 2 * ring, ring) // (ring // 2)

    here = heads_at(0)
    seq_of_side = (1 - here, here)

    is_top = work == segments - 1
    edge_src = (z == 0) & (work_run > 0)
    edge_dst = (z == RUN - 1) & (work < segments - 1)
    helper = (z > 0) & (work_run > 0)
    plain_src = z > 0
    plain_dst = z < RUN - 1
    lender = run == segments // RUN - 1
    borne = HELPERS
    early = heads // 2

    def at(section):
        return {"segment": section}

    def signal(sem, device):
        pl.semaphore_signal(sem, inc=1, device_id=device, device_id_type=MESH)

    barrier = pltpu.get_barrier_semaphore()
    for dy in sides:
        signal(barrier, place(dy))
    local = [
        pltpu.make_async_copy(tab_ref.at[0, :, 0], table, lsem.at[0]),
        pltpu.make_async_copy(cnt_ref.at[0, :, 0], count, lsem.at[1]),
        pltpu.make_async_copy(sf_ref.at[0], sfv, lsem.at[2]),
    ]
    for c in local:
        c.start()

    @pl.when(plain_dst)
    def _():
        signal(barrier, at(seg + 1))

    @pl.when(edge_src)
    def _():
        signal(barrier, place(-1, RUN - 1))
        for k in range(1, HELPERS + 1):
            signal(barrier, at(lax.rem(seg + k, segments)))

    @pl.when(helper)
    def _():
        signal(barrier, place(-1, RUN - 1))

    top_at = {"segment": segments // 2 - 1, "seq": 1 - seq}

    @pl.when(lender)
    def _():
        signal(barrier, top_at)

    back = jnp.where(z == 0, 1, 0)
    line = lax.rem(y + ring - back, ring)
    turn = lax.rem(dp + n_dp - back, n_dp)

    def greet(t, carry):
        signal(barrier, place(0, None, lax.rem(t + back, n_dp)))
        return carry

    lax.fori_loop(turn + 1, n_dp, greet, 0)
    higher = [lax.rem(line + dy + ring, ring) > line for dy in sides]
    for dy, up in zip(sides, higher):
        @pl.when(up)
        def _():
            for d in range(1, n_dp):
                signal(barrier, place(dy, None, lax.rem(dp + d, n_dp)))

    def one(cond, amount=1):
        return jnp.where(cond, amount, 0)

    pl.semaphore_wait(
        barrier,
        2 + turn + sum(one(~up, n_dp - 1) for up in higher) + one(plain_src)
        + one(edge_dst, 1 + HELPERS) + one(helper) + one(is_top, LENDERS),
    )

    def cols_of(group, h):
        return pl.ds(pl.multiple_of((group * heads + h) * HEAD_DIM, HEAD_DIM), HEAD_DIM)

    def send_x(w, k, h):
        dy = (reach, -reach)[k]
        return pltpu.make_async_remote_copy(
            src_ref=x_ref.at[0, w, 0, :, cols_of(heads_at(dy), h)], dst_ref=x_in.at[w, k, h],
            send_sem=x_s.at[w, k, h], recv_sem=x_r.at[w, k, h],
            device_id=place(dy), device_id_type=MESH,
        )

    def send_p(k, h):
        dy = (reach, -reach)[k]
        return pltpu.make_async_remote_copy(
            src_ref=p_ref.at[0, 0, :, cols_of(heads_at(dy), h)], dst_ref=p_in.at[k, h],
            send_sem=p_s.at[k, h], recv_sem=p_r.at[k, h],
            device_id=place(dy), device_id_type=MESH,
        )

    def send_meta():
        return pltpu.make_async_remote_copy(
            src_ref=meta, dst_ref=meta_in, send_sem=m_s.at[0], recv_sem=m_r.at[0],
            device_id=place(reach), device_id_type=MESH,
        )

    def send_u(h):
        return pltpu.make_async_remote_copy(
            src_ref=u_ref.at[0, 0, :, cols_of(1 - seq, h)], dst_ref=arr.at[h, pl.ds(0, BLK)],
            send_sem=u_s.at[h], recv_sem=down_r.at[h], device_id=top_at, device_id_type=MESH,
        )

    def own_u(h):
        return pltpu.make_async_copy(
            u_ref.at[0, 0, :, cols_of(here, h)], arr.at[h, pl.ds(BLK, BLK)], lsem.at[3 + h]
        )

    def send_down(h):
        return pltpu.make_async_remote_copy(
            src_ref=gin.at[h], dst_ref=arr.at[h],
            send_sem=down_s.at[h], recv_sem=down_r.at[h],
            device_id=at(lax.rem(seg + segments - 1, segments)), device_id_type=MESH,
        )

    def send_edge(h):
        return pltpu.make_async_remote_copy(
            src_ref=gin.at[h], dst_ref=arr.at[h],
            send_sem=down_s.at[h], recv_sem=down_r.at[h],
            device_id=place(-1, RUN - 1), device_id_type=MESH,
        )

    def send_helper(h):
        return pltpu.make_async_remote_copy(
            src_ref=gin.at[h], dst_ref=passing,
            send_sem=down_s.at[h], recv_sem=pass_r.at[0],
            device_id=at(lax.rem(seg + 1 + h, segments)), device_id_type=MESH,
        )

    def send_on():
        return pltpu.make_async_remote_copy(
            src_ref=passing, dst_ref=arr.at[z - 1],
            send_sem=pass_s.at[0], recv_sem=down_r.at[z - 1],
            device_id=place(-1, RUN - 1), device_id_type=MESH,
        )

    for h in range(LOOK):
        for k in range(2):
            send_x(0, k, h).start()
            send_p(k, h).start()

    for c in local:
        c.wait()
    ahead = heads_at(reach)
    for h in range(heads):
        cols = cols_of(ahead, h)
        meta[h : h + 1] = sfv[0:1, cols] * sfv[1:2, cols]
        meta[heads + h : heads + h + 1] = sfv[3:4, cols] * sfv[2:3, cols]
    for w in range(2):
        for c in range(2):
            for a in range(2):
                hit = (table[w, a, 0] == c) | ((count[w, a] > 1) & (table[w, a, 1] == c))
                row = 2 * heads + 4 * w + 2 * c + a
                value = jnp.where(hit, 0.0, MASKED).astype(jnp.float32)
                meta[row : row + 1] = jnp.full((1, HEAD_DIM), value, jnp.float32)
    send_meta().start()

    @pl.when(edge_dst)
    def _():
        for k in range(HELPERS + 1):
            signal(ready.at[0], place(1, k))

    @pl.when(helper)
    def _():
        signal(ready.at[2 + z], at(seg - z))

    @pl.when(is_top)
    def _():
        for k in range(LENDERS):
            signal(ready.at[1], {"segment": segments - RUN + k, "seq": 1 - seq})

    def answer(t, carry):
        signal(ready.at[2], place(0, None, lax.rem(t + back, n_dp)))
        return carry

    lax.fori_loop(0, turn, answer, 0)
    for dy, up in zip(sides, higher):
        @pl.when(~up)
        def _():
            for d in range(1, n_dp):
                signal(ready.at[2], place(dy, None, lax.rem(dp + d, n_dp)))

    later = n_dp - 1 - turn + sum(one(up, n_dp - 1) for up in higher)

    def bias_of(w):
        rows = []
        for c in range(2):
            base = 2 * heads + 4 * w + 2 * seq_of_side[c]
            rows.append(
                jnp.concatenate(
                    [meta_in[pl.ds(base + seq_of_side[r], 1)] for r in range(2)], axis=1
                )
            )
        return rows

    def first_batch(h, carry):
        for k in range(2):
            send_x(0, k, h).wait_send()
            send_p(k, h).wait_send()

            @pl.when(h + LOOK < heads)
            def _():
                send_x(0, k, h + LOOK).start()
                send_p(k, h + LOOK).start()

            @pl.when(h + LOOK >= heads)
            def _():
                first = (h + LOOK - heads) * 2
                send_x(1, k, first).start()
                send_x(1, k, first + 1).start()

        @pl.when(is_top)
        def _():
            own_u(h).start()

        @pl.when(lender & (h == heads - 1 - z))
        def _():
            pl.semaphore_wait(ready.at[1], 1)
            send_u(h).start()

        @pl.when(h == 0)
        def _():
            send_meta().wait_recv()

        for k in range(2):
            send_x(0, k, h).wait_recv()
            send_p(k, h).wait_recv()
        x = jnp.concatenate([x_in[0, 0, h], x_in[0, 1, h]], axis=0)
        pend = jnp.concatenate([p_in[0, h], p_in[1, h]], axis=0)
        key_sum, val_sum, grad_input = head_math(
            x, pend, meta_in[pl.ds(h, 1)], meta_in[pl.ds(heads + h, 1)], bias_of(0), True
        )
        gin[h] = grad_input

        @pl.when(plain_src)
        def _():
            send_down(h).start()

        @pl.when(edge_src & (h < borne))
        def _():
            pl.semaphore_wait(ready.at[3 + h], 1)
            send_helper(h).start()

        @pl.when(edge_src & (h == borne))
        def _():
            pl.semaphore_wait(ready.at[0], 1)
            send_edge(h).start()

        @pl.when(helper & (h == jnp.minimum(jnp.maximum(z + 1, 5), heads - 1)))
        def _():
            pl.semaphore_wait(ready.at[0], 1)
            send_helper(z - 1).wait_recv()
            send_on().start()

        @pl.when(h < early)
        def _():
            part[h] = key_sum
            part[early + h] = val_sum

        @pl.when(h >= early)
        def _():
            late[pl.ds(h - early, 1)] = key_sum
            late[pl.ds(h, 1)] = val_sum

        return carry

    lax.fori_loop(0, heads, first_batch, 0)

    def send_part(d):
        to = lax.rem(dp + d, n_dp)
        return pltpu.make_async_remote_copy(
            src_ref=part.at[to], dst_ref=coll.at[dp],
            send_sem=one_s.at[d], recv_sem=one_r.at[d], device_id={"dp": to}, device_id_type=MESH,
        )

    def send_mid(k, d):
        return pltpu.make_async_remote_copy(
            src_ref=tot, dst_ref=mid.at[here, dp],
            send_sem=two_s.at[k, d], recv_sem=two_r.at[k, d],
            device_id=place(sides[k], None, lax.rem(dp + d, n_dp)), device_id_type=MESH,
        )

    def send_late(k, d):
        return pltpu.make_async_remote_copy(
            src_ref=late, dst_ref=gath.at[here, dp],
            send_sem=red_s.at[k, d], recv_sem=red_r.at[k, d],
            device_id=place(sides[k], None, lax.rem(dp + d, n_dp)), device_id_type=MESH,
        )

    order = [(k, d) for d in (4, 3, 5, 2, 6, 1, 7, 0) for k in range(2)]

    def second_batch(h, carry):
        for k in range(2):
            send_x(1, k, h).wait_recv()

        @pl.when(is_top)
        def _():
            own_u(h).wait()
            send_u(h).wait_recv()

        @pl.when(work < segments - 1)
        def _():
            send_down(h).wait_recv()

        x = jnp.concatenate([x_in[1, 0, h], x_in[1, 1, h]], axis=0)
        key_sum, val_sum, _ = head_math(
            x, arr[h], meta_in[pl.ds(h, 1)], meta_in[pl.ds(heads + h, 1)], bias_of(1), False
        )

        @pl.when(h < early)
        def _():
            part[h] += key_sum
            part[early + h] += val_sum

        @pl.when(h >= early)
        def _():
            late[pl.ds(h - early, 1)] += key_sum
            late[pl.ds(h, 1)] += val_sum

        @pl.when(h == early - 1)
        def _():
            @pl.when(later > 0)
            def _():
                pl.semaphore_wait(ready.at[2], later)

            coll[dp] = part[dp]
            for d in range(1, n_dp):
                send_part(d).start()

        return carry

    lax.fori_loop(0, heads, second_batch, 0)

    for k, d in order:
        send_late(k, d).start()
    for d in range(1, n_dp):
        send_part(d).wait_recv()
    total = coll[0]
    for d in range(1, n_dp):
        total = total + coll[d]
    tot[...] = total
    for k, d in order:
        send_mid(k, d).start()
    def write(s, h, key_sum, val_sum):
        cols = slice((s * heads + h) * HEAD_DIM, (s * heads + h + 1) * HEAD_DIM)
        out_ref[0, 0:1, cols] = sfv[1:2, cols] * key_sum
        out_ref[0, 1:2, cols] = sfv[0:1, cols] * key_sum
        out_ref[0, 2:3, cols] = sfv[3:4, cols] * val_sum
        out_ref[0, 3:4, cols] = sfv[2:3, cols] * val_sum

    for k, d in order:
        send_late(k, d).wait_recv()
    for s in range(2):
        total = gath[s, 0]
        for d in range(1, n_dp):
            total = total + gath[s, d]
        for h in range(early, heads):
            write(s, h, total[h - early : h - early + 1], total[h : h + 1])
    for k, d in order:
        send_mid(k, d).wait_recv()
    for s in range(2):
        for h in range(early):
            write(s, h, mid[s, h], mid[s, early + h])

    def drain_down(h, carry):
        for k in range(2):
            send_x(1, k, h).wait_send()

        @pl.when(plain_src | edge_src)
        def _():
            send_down(h).wait_send()

        @pl.when(lender & (h == heads - 1 - z))
        def _():
            send_u(h).wait_send()

        return carry

    lax.fori_loop(0, heads, drain_down, 0)

    @pl.when(helper)
    def _():
        send_on().wait_send()

    send_meta().wait_send()
    for d in range(1, n_dp):
        send_part(d).wait_send()
    for k, d in order:
        send_mid(k, d).wait_send()
        send_late(k, d).wait_send()


def shards(segments, n_dp, x, pend, top, gains, table, count):
    rows, channels = x.shape[3], x.shape[4]
    heads = channels // HEAD_DIM // 2
    in_place = pl.BlockSpec(memory_space=pltpu.HBM)
    dma = pltpu.SemaphoreType.DMA
    low = jnp.bfloat16
    return pl.pallas_call(
        functools.partial(sweep_kernel, segments, n_dp, heads),
        out_shape=jax.ShapeDtypeStruct((1, 4, channels), jnp.float32),
        in_specs=[in_place] * 6,
        out_specs=pl.BlockSpec(memory_space=pltpu.VMEM),
        scratch_shapes=[
            pltpu.VMEM((2, 2, heads, rows, HEAD_DIM), low),
            pltpu.VMEM((2, heads, rows, HEAD_DIM), low),
            pltpu.VMEM((heads, 2 * rows, HEAD_DIM), low),
            pltpu.VMEM((heads, 2 * rows, HEAD_DIM), low),
            pltpu.VMEM((2 * rows, HEAD_DIM), low),
            pltpu.VMEM((4, channels), jnp.float32),
            pltpu.VMEM((2 * heads + 8, HEAD_DIM), jnp.float32),
            pltpu.VMEM((2 * heads + 8, HEAD_DIM), jnp.float32),
            pltpu.VMEM((n_dp, 1, HEAD_DIM), jnp.float32),
            pltpu.VMEM((heads, HEAD_DIM), jnp.float32),
            pltpu.VMEM((n_dp, 1, HEAD_DIM), jnp.float32),
            pltpu.VMEM((1, HEAD_DIM), jnp.float32),
            pltpu.VMEM((2, n_dp, 1, HEAD_DIM), jnp.float32),
            pltpu.VMEM((2, n_dp, heads, HEAD_DIM), jnp.float32),
            pltpu.SMEM((2, 2, 2), jnp.int32),
            pltpu.SMEM((2, 2), jnp.int32),
            dma((3 + heads,)),
            dma((2, 2, heads)),
            dma((2, 2, heads)),
            dma((2, heads)),
            dma((2, heads)),
            dma((1,)),
            dma((1,)),
            dma((heads,)),
            dma((heads,)),
            dma((heads,)),
            dma((1,)),
            dma((1,)),
            dma((n_dp,)),
            dma((n_dp,)),
            dma((2, n_dp)),
            dma((2, n_dp)),
            dma((2, n_dp)),
            dma((2, n_dp)),
            pltpu.SemaphoreType.REGULAR((3 + HELPERS,)),
        ],
        compiler_params=pltpu.CompilerParams(
            collective_id=1, has_side_effects=True, vmem_limit_bytes=32 << 20
        ),
        name="sweep",
    )(*[pltpu.with_memory_space_constraint(v, pltpu.HBM) for v in (x, pend, top, gains, table, count)])


def solution(mesh):
    placed = (
        P("segment", None, "dp", "seq", None),
        P("segment", "dp", "seq", None),
        P(None, "dp", "seq", None),
        P("segment", None, None),
        P("segment", None, "dp", None, None),
        P("segment", None, "dp", None),
    )
    body = functools.partial(shards, mesh.shape["segment"], mesh.shape["dp"])
    return jax.shard_map(
        body, mesh=mesh, in_specs=placed, out_specs=P("segment", None, None), check_vma=False
    )
```
